32 devices in a mesh: tm: 4 (over x, core), chan: 8 (over z, y).
Axes of the slice: x: 2, y: 2, z: 4, core: 2. Of those that a mesh axis runs over, the one named last changes fastest.
Arguments:
- raw_blocks: bfloat16 [16, 5120, 1024], P('tm', 'chan'), may hold values from -6 to 6
- fir_taps: bfloat16 [128], replicated, may hold values from -0.5 to 0.5
- recorder_channel: int32 [5120], replicated, may hold values from 0 to 5119, as said below
- pairs: int32 [4096, 2], P('chan'), may hold values from 0 to 5119, as said below
Outputs:
- stacks: float32 [4096, 256], P('chan')
The draws below stay inside these ranges and needn't reach their ends.
Inputs may be any that keep to these rules, and one draw needn't show every extreme that they name: `recorder_channel`: A permutation of the channels; each aligned block of 640 recorder rows holds exactly 80 channels of every range of 640 consecutive channels. `pairs`: each aligned block of 512 rows names exactly 32 distinct channels of every range of 640 consecutive channels.
All inputs are finite; a program needn't handle non-finite values.
Results may differ from the reference program's by a relative error of at most 0.0084.
Values may be sent and summed in bfloat16 or wider, within the bound.
No kernel may reach another device: no remote copies, remote signals or barrier semaphores. Data moves between devices by JAX's collectives and lax.ppermute only.
A program may use at most 128 MiB of HBM per device.

```python
import jax
import jax.numpy as jnp
from jax import lax

L = 1024
TAPS = 128
NB = 128
SMOOTH = 4
CH_DEV = 640
P_DEV = 512
Q = 32
CH = 5120
NWIN = 16
PAIRS = 4096


def draw_recorder_channel(key, part):
    owners = CH // CH_DEV
    per_group = CH_DEV // owners
    subkeys = jax.random.split(key, owners)
    shuffles = jax.vmap(lambda sub: jax.random.permutation(sub, CH_DEV))(subkeys).astype(jnp.int32)
    channel_ids = shuffles + (jnp.arange(owners, dtype=jnp.int32) * CH_DEV)[:, None]
    blocks = channel_ids.reshape(owners, owners, per_group).transpose(1, 0, 2).reshape(owners, CH_DEV)
    second_keys = jax.random.split(jax.random.fold_in(key, 7), owners)
    mixed = jax.vmap(lambda sub, row_ids: jax.random.permutation(sub, row_ids))(second_keys, blocks)
    return mixed.reshape(CH).astype(jnp.int32)


def owner_pairs(sub):
    owners = CH // CH_DEV
    pool_size = owners * Q
    extra_count = 2 * P_DEV - pool_size
    pick_keys = jax.random.split(jax.random.fold_in(sub, 1), owners)
    chosen = jax.vmap(lambda kk: jax.random.permutation(kk, CH_DEV)[:Q])(pick_keys).astype(jnp.int32)
    channel_pool = (chosen + (jnp.arange(owners, dtype=jnp.int32) * CH_DEV)[:, None]).reshape(pool_size)
    channel_pool = jax.random.permutation(jax.random.fold_in(sub, 2), channel_pool)
    draw_one = jax.random.randint(jax.random.fold_in(sub, 3), (extra_count,), 0, pool_size)
    draw_two = jax.random.randint(jax.random.fold_in(sub, 4), (extra_count,), 0, pool_size)
    extra = channel_pool[jnp.minimum(draw_one, draw_two)]
    endpoints = jnp.concatenate([channel_pool, extra])
    endpoints = jax.random.permutation(jax.random.fold_in(sub, 5), endpoints)
    return endpoints.reshape(P_DEV, 2)


def draw_pairs(key, part):
    owners = CH // CH_DEV
    subkeys = jax.random.split(jax.random.fold_in(key, 11), owners)
    return jax.vmap(owner_pairs)(subkeys).reshape(PAIRS, 2).astype(jnp.int32)


def block_scale(rng, dims, shards, smallest, top_value):
    def one(position, blocks):
        steps = jax.random.uniform(jax.random.fold_in(jax.random.fold_in(rng, 6), position), (blocks,), jnp.float32, smallest / len(shards), top_value / len(shards))
        return jnp.repeat(jnp.exp(steps), dims[position] // blocks).reshape((-1,) + (1,) * (len(dims) - position - 1))

    loudness = one(*shards[0])
    for cut in shards[1:]:
        loudness = loudness * one(*cut)
    return loudness


def noise(rng, dims, spread, reach, cuts=(), held_as=jnp.bfloat16):
    result = spread * jax.random.normal(rng, dims, jnp.float32)
    if cuts:
        result = result * block_scale(rng, dims, cuts, -0.22, 0.18)
    return jnp.clip(result, -reach, reach).astype(held_as)


def setup_inputs(seed: int = 0) -> dict:
    splits = jax.random.split(jax.random.key(seed), 5)
    raw_blocks = noise(splits[0], (NWIN, CH, L), 1.0, 6.0, ((0, 4), (1, 8)))
    fir_taps = noise(splits[1], (TAPS,), TAPS ** -0.5, 0.5)
    recorder_channel = draw_recorder_channel(jax.random.fold_in(splits[4], 71), 0)
    pairs = draw_pairs(jax.random.fold_in(splits[4], 71), 0)
    return dict(raw_blocks=raw_blocks, fir_taps=fir_taps, recorder_channel=recorder_channel, pairs=pairs)


def make_fir(fir_taps, length):
    taps_n = fir_taps.shape[0]
    period = taps_n + length
    padded = jnp.concatenate([fir_taps.astype(jnp.float32), jnp.zeros((length,), jnp.float32)])
    repeated = jnp.tile(padded, length)[:length * (period - 1)].reshape(length, period - 1)[:, :length]
    return repeated.astype(jnp.bfloat16)

def make_table(length, bin_count):
    samples = jnp.arange(length, dtype=jnp.int32)
    freqs = jnp.arange(1, bin_count + 1, dtype=jnp.int32)
    phase_idx = samples[:, None] * freqs[None, :] % length
    angles = phase_idx.astype(jnp.float32) * (2.0 * jnp.pi / length)
    return jnp.concatenate([jnp.cos(angles), -jnp.sin(angles)], axis=1).astype(jnp.bfloat16)

def make_smooth(bin_count, half_width):
    places = jnp.arange(bin_count, dtype=jnp.int32)
    band_mask = (jnp.abs(places[:, None] - places[None, :]) <= half_width).astype(jnp.float32)
    return band_mask / lax.optimization_barrier(jnp.sum(band_mask, axis=0, keepdims=True))

def whiten(spectrum, smoother):
    bin_count = spectrum.shape[-1] // 2
    real_part = spectrum[..., :bin_count]
    imag_part = spectrum[..., bin_count:]
    magnitude = jnp.sqrt(real_part * real_part + imag_part * imag_part)
    smoothed = jnp.dot(magnitude, smoother, precision=lax.Precision.HIGHEST)
    mean_level = lax.optimization_barrier(jnp.mean(magnitude, axis=-1, keepdims=True))
    divisor = smoothed + 0.1 * mean_level + 1e-06
    return (spectrum / jnp.concatenate([divisor, divisor], axis=-1)).astype(jnp.bfloat16)

def cross(left_rows, right_rows):
    bin_count = left_rows.shape[-1] // 2
    left_f = left_rows.astype(jnp.float32)
    right_f = right_rows.astype(jnp.float32)
    left_re, left_im = (left_f[..., :bin_count], left_f[..., bin_count:])
    right_re, right_im = (right_f[..., :bin_count], right_f[..., bin_count:])
    real_out = left_re * right_re + left_im * right_im
    imag_out = left_im * right_re - left_re * right_im
    return jnp.concatenate([real_out, imag_out], axis=-1)

def reference(raw_blocks, fir_taps, recorder_channel, pairs):
    rows_of = jnp.argsort(recorder_channel, stable=True).astype(jnp.int32)
    left_idx = rows_of[pairs[:, 0]]
    right_idx = rows_of[pairs[:, 1]]
    fir_matrix = make_fir(fir_taps, L)
    dft_table = make_table(L, NB)
    smoother = make_smooth(NB, SMOOTH)

    def advance(summed, window_rows):
        filtered = jnp.dot(window_rows, fir_matrix, preferred_element_type=jnp.float32).astype(jnp.bfloat16)
        spectrum = jnp.dot(filtered, dft_table, preferred_element_type=jnp.float32)
        whitened = whiten(spectrum, smoother)
        return (summed + cross(whitened[left_idx], whitened[right_idx]), None)
    summed, _ = lax.scan(advance, jnp.zeros((PAIRS, 2 * NB), jnp.float32), raw_blocks)
    return summed / NWIN
```

```python
import functools

import jax
import jax.numpy as jnp
import ml_dtypes
import numpy as np
from jax import lax
from jax.experimental import pallas as pl
from jax.experimental.pallas import tpu as pltpu
from jax.sharding import PartitionSpec as P

NB = 128
SMOOTH = 4
LANES = 128
ROUND_ROWS = 48

F32, BF16, I32 = jnp.float32, jnp.bfloat16, jnp.int32
VMEM = pl.BlockSpec(memory_space=pltpu.VMEM)
SMEM = pl.BlockSpec(memory_space=pltpu.SMEM)
NT = (((1,), (1,)), ((), ()))


def table_of(length, pad):
    samples = np.arange(length, dtype=np.int64)
    freqs = np.arange(1, NB + 1, dtype=np.int64)
    phase = (samples[:, None] * freqs[None, :] % length).astype(np.float32)
    angles = (phase * np.float32(2.0 * np.pi / length)).astype(np.float64)
    table = np.concatenate([np.cos(angles), -np.sin(angles)], axis=1).astype(np.float32)
    table = np.concatenate([table, np.zeros((pad, 2 * NB), np.float32)])
    return table.astype(ml_dtypes.bfloat16)


def smoothing_of():
    places = np.arange(NB)
    band = (np.abs(places[:, None] - places[None, :]) <= SMOOTH).astype(np.float32)
    both = np.concatenate([band, np.ones((NB, NB), np.float32)], axis=1)
    stacked = np.concatenate([both, both], axis=0).astype(ml_dtypes.bfloat16)
    return stacked, (1.0 / band.sum(axis=0, keepdims=True)).astype(np.float32)


def dot(a, b, dims=(((1,), (0,)), ((), ()))):
    return lax.dot_general(a, b, dims, preferred_element_type=F32)


def iota(shape, axis):
    return lax.broadcasted_iota(I32, shape, axis)


def combine_kernel(taps_ref, table_ref, out_ref):
    taps = taps_ref[...].astype(F32)
    n = taps.shape[1]
    wide = jnp.concatenate([taps, jnp.zeros_like(taps)], axis=1)
    toeplitz = pltpu.roll(jnp.broadcast_to(wide, (n, 2 * n)), 0, 1, stride=1, stride_axis=0)
    toeplitz = toeplitz.astype(BF16)
    for b in range(out_ref.shape[0] // n):
        rows = table_ref[b * n : (b + 2) * n, :]
        out_ref[b * n : (b + 1) * n, :] = dot(toeplitz, rows).astype(BF16)


def spectrum_kernel(core_ref, raw_ref, mat_ref, sum_ref, inv_ref, keep_ref, give_ref):
    spec = dot(raw_ref[0], mat_ref[...])
    re, im = spec[:, :NB], spec[:, NB:]
    mag = jnp.sqrt(re * re + im * im)
    high = mag.astype(BF16)
    low = (mag - high.astype(F32)).astype(BF16)
    sums = dot(jnp.concatenate([high, low], axis=1), sum_ref[...])
    divisor = sums[:, :NB] * inv_ref[...] + sums[:, NB:] * (0.1 / NB) + 1e-06
    scale = 1.0 / divisor
    re = re * scale
    im = im * scale
    half = NB // 2
    left = iota(re.shape, 1) < half
    first = jnp.where(left, re, pltpu.roll(im, half, 1)).astype(BF16)
    second = jnp.where(left, pltpu.roll(re, half, 1), im).astype(BF16)
    core = core_ref[0]

    @pl.when(core == 0)
    def _():
        keep_ref[0] = first
        give_ref[0] = second

    @pl.when(core != 0)
    def _():
        keep_ref[0] = second
        give_ref[0] = first


def one_hots(ids, high_count):
    width = ids.shape[1]
    high = (iota((high_count, width), 0) == ids // LANES).astype(F32).astype(BF16)
    low = (iota((LANES, width), 0) == ids % LANES).astype(F32).astype(BF16)
    return high, low


def before(count):
    return (iota((count, count), 0) < iota((count, count), 1)).astype(F32).astype(BF16)


def pack_kernel(n, me_ref, pairs_ref, chan_ref, keep_ref, other_ref, place_ref, *chunk_refs):
    rows = chan_ref.shape[1]
    high_count = n * rows // LANES
    high_r, low_r = one_hots(chan_ref[pl.ds(me_ref[0], 1), :], high_count)
    low_r = low_r.astype(F32)
    wants = []
    for k in range(n):
        table = None
        for j in range(2):
            high_e, low_e = one_hots(pairs_ref[2 * k + j : 2 * k + j + 1, :], high_count)
            part = dot(low_e, high_e, NT)
            table = part if table is None else table + part
        table = (table > 0.5).astype(F32).astype(BF16)
        wants.append(jnp.sum(dot(table, high_r) * low_r, axis=0, keepdims=True))
    want = jnp.concatenate(wants, axis=0)
    place = dot(want.astype(BF16), before(rows))
    place = jnp.where(want > 0.5, place, -1.0).astype(I32)
    place_ref[...] = place
    chunk = chunk_refs[0].shape[0]
    slots = iota((chunk, rows), 0)
    select = jnp.concatenate([(slots == place[k : k + 1, :]).astype(F32).astype(BF16) for k in range(n)])
    windows = keep_ref.shape[0]
    for w in range(windows):
        data = jnp.concatenate([keep_ref[w], other_ref[w]], axis=1)
        out = dot(select, data).astype(BF16)
        for k in range(n):
            chunk_refs[k][:, 2 * w * LANES : 2 * (w + 1) * LANES] = out[k * chunk : (k + 1) * chunk]


def arrival_kernel(n, chunk, me_ref, pairs_ref, chan_ref, ends_ref, gather_ref, where_ref, most_ref):
    rows = chan_ref.shape[1]
    high_count = n * rows // LANES
    me = me_ref[0]
    tables = []
    for k in range(n):
        table = None
        for j in range(2):
            high_e, low_e = one_hots(pairs_ref[2 * k + j : 2 * k + j + 1, :], high_count)
            part = dot(high_e, low_e, NT)
            table = part if table is None else table + part
        tables.append((table > 0.5).astype(F32))
    mine = tables[0].T.astype(BF16)
    held, wants, hots = [], [], []
    for s in range(n):
        high_s, low_s = one_hots(chan_ref[s : s + 1, :], high_count)
        hots.append((high_s, low_s))
        held.append(dot(high_s, low_s, NT).astype(BF16))
        wants.append(jnp.sum(dot(mine, high_s) * low_s.astype(F32), axis=0, keepdims=True))
    place = dot(jnp.concatenate(wants, axis=0).astype(BF16), before(rows)).astype(I32)
    planes = [None] * 3
    for s in range(n):
        high_s, low_s = hots[s]
        at = place[s : s + 1, :]
        source = jnp.full(at.shape, s ^ me, I32)
        for i, value in enumerate((source, at // LANES, at % LANES)):
            part = dot(high_s, (low_s.astype(F32) * value.astype(F32)).astype(BF16), NT)
            planes[i] = part if planes[i] is None else planes[i] + part
    ends = ends_ref[...]
    count = ends.shape[0]
    high_e = (iota((count, high_count), 1) == ends // LANES).astype(F32).astype(BF16)
    low_e = (iota((count, LANES), 1) == ends % LANES).astype(F32)
    found = [jnp.sum(dot(high_e, p.astype(BF16)) * low_e, axis=1, keepdims=True) for p in planes]
    source = found[0].astype(I32)
    at = (found[1] * LANES + found[2]).astype(I32)
    where_ref[...] = jnp.where(iota((count, 2), 1) == 0, source, at)
    slot = jnp.where(at < chunk, source * chunk + at, -1)
    gather_ref[...] = (iota(gather_ref.shape, 1) == slot).astype(F32).astype(BF16)
    tables = jnp.concatenate(tables, axis=0).astype(BF16)
    cross = dot(jnp.concatenate(held, axis=0), tables, NT)
    shape = cross.shape
    cross = jnp.where(iota(shape, 0) % high_count == iota(shape, 1) % high_count, cross, 0.0)
    block = (iota((n, shape[0]), 1) // high_count == iota((n, shape[0]), 0)).astype(F32).astype(BF16)
    sums = dot(block, cross.astype(BF16))
    owner = iota(sums.shape, 1) // high_count
    most = jnp.zeros((n, 1), F32)
    for p in range(n):
        most = jnp.maximum(most, jnp.sum(jnp.where(owner == p, sums, 0.0), axis=1, keepdims=True))
    most_ref[...] = jnp.max(most, axis=0, keepdims=True).astype(I32)


def pair_products(left, right):
    windows = left.shape[1] // LANES
    half = LANES // 2
    straight = crossed = None
    for w in range(windows):
        a = left[:, w * LANES : (w + 1) * LANES]
        b = right[:, w * LANES : (w + 1) * LANES]
        turned = pltpu.roll(a, half, 1)
        straight = a * b if straight is None else straight + a * b
        crossed = turned * b if crossed is None else crossed + turned * b
    real = straight + pltpu.roll(straight, half, 1)
    imag = pltpu.roll(crossed, half, 1) - crossed
    return jnp.where(iota(real.shape, 1) < half, real, imag)


def product_kernel(n, gather_ref, *refs):
    chunk_refs, out_ref, rows_ref = refs[:n], refs[n], refs[n + 1]
    chunk = chunk_refs[0].shape[0]
    for k in range(n):
        rows_ref[k * chunk : (k + 1) * chunk, :] = chunk_refs[k][...]
    pair_count = out_ref.shape[0]
    step = 128
    for p in range(0, pair_count, step):
        left = dot(gather_ref[p : p + step, :], rows_ref[...])
        right = dot(gather_ref[pair_count + p : pair_count + p + step, :], rows_ref[...])
        out_ref[p : p + step, :] = pair_products(left, right).astype(out_ref.dtype)


def finish_kernel(factor, core_ref, mine_ref, other_ref, out_ref):
    mine = mine_ref[...] * factor
    other = other_ref[...] * factor
    first_core = core_ref[0] == 0
    first = jnp.where(first_core, mine, other)
    second = jnp.where(first_core, other, mine)
    half = LANES // 2
    left = iota(first.shape, 1) < half
    out_ref[:, :LANES] = jnp.where(left, first, pltpu.roll(second, half, 1))
    out_ref[:, LANES:] = jnp.where(left, pltpu.roll(first, half, 1), second)


def swap(value, axis, size, bit):
    return lax.ppermute(value, axis, [(i, i ^ bit) for i in range(size)])


def local(tm, n, raw_blocks, fir_taps, recorder_channel, pairs):
    windows, rows, length = raw_blocks.shape
    pair_count = pairs.shape[0]
    chunk = ROUND_ROWS
    params = pltpu.CompilerParams(vmem_limit_bytes=48 * 1024 * 1024)
    me = lax.axis_index("chan").astype(I32).reshape(1)
    core = (lax.axis_index("tm") % 2).astype(I32).reshape(1)

    table = jnp.asarray(table_of(length, fir_taps.shape[0]))
    sum_np, inv_np = smoothing_of()
    matrix = pl.pallas_call(
        combine_kernel,
        out_shape=jax.ShapeDtypeStruct((length, 2 * NB), BF16),
        in_specs=[VMEM, VMEM],
        out_specs=VMEM,
        name="combine",
        compiler_params=params,
    )(fir_taps.reshape(1, -1), table)

    bands = 2
    part = rows // bands
    half_shape = jax.ShapeDtypeStruct((windows, rows, NB), BF16)
    half_spec = pl.BlockSpec((1, part, NB), lambda w, b: (w, b, 0))
    keep, give = pl.pallas_call(
        spectrum_kernel,
        out_shape=(half_shape, half_shape),
        grid=(windows, bands),
        in_specs=[
            SMEM,
            pl.BlockSpec((1, part, length), lambda w, b: (w, b, 0)),
            pl.BlockSpec((length, 2 * NB), lambda w, b: (0, 0)),
            pl.BlockSpec((2 * NB, 2 * NB), lambda w, b: (0, 0)),
            pl.BlockSpec((1, NB), lambda w, b: (0, 0)),
        ],
        out_specs=(half_spec, half_spec),
        name="spectrum",
        compiler_params=params,
        cost_estimate=pl.CostEstimate(
            flops=2 * windows * rows * length * 2 * NB,
            bytes_accessed=2 * windows * rows * (length + 2 * NB),
            transcendentals=0,
        ),
    )(core, raw_blocks, matrix, jnp.asarray(sum_np), jnp.asarray(inv_np))
    other = swap(give, "tm", tm, 1)

    everyone = pairs.T.reshape(1, 2, pair_count)
    order = [0]
    bit = 1
    while bit < n:
        everyone = jnp.concatenate([everyone, swap(everyone, "chan", n, bit)])
        order = order + [k ^ bit for k in order]
        bit *= 2
    everyone = everyone.reshape(2 * n, pair_count)
    by_block = recorder_channel.reshape(n, rows)

    chunk_shape = jax.ShapeDtypeStruct((chunk, 2 * windows * LANES), BF16)
    place, *chunks = pl.pallas_call(
        functools.partial(pack_kernel, n),
        out_shape=(jax.ShapeDtypeStruct((n, rows), I32),) + (chunk_shape,) * n,
        in_specs=[SMEM, VMEM, VMEM, VMEM, VMEM],
        out_specs=(VMEM,) * (n + 1),
        name="pack",
        compiler_params=params,
    )(me, everyone, by_block, keep, other)

    arrived = [chunks[0]] + [swap(chunks[k], "chan", n, k) for k in range(1, n)]

    ends = pairs.T.reshape(2 * pair_count, 1)
    gather, found, most = pl.pallas_call(
        functools.partial(arrival_kernel, n, chunk),
        out_shape=(
            jax.ShapeDtypeStruct((2 * pair_count, n * chunk), BF16),
            jax.ShapeDtypeStruct((2 * pair_count, 2), I32),
            jax.ShapeDtypeStruct((1, 1), I32),
        ),
        in_specs=[SMEM, VMEM, VMEM, VMEM],
        out_specs=(VMEM,) * 3,
        name="arrival",
        compiler_params=params,
    )(me, everyone, by_block, ends)
    most = most[0, 0]

    def one_round(ops):
        gather, arrived = ops[0], ops[1]
        return pl.pallas_call(
            functools.partial(product_kernel, n),
            out_shape=jax.ShapeDtypeStruct((pair_count, LANES), BF16),
            in_specs=[VMEM] * (n + 1),
            out_specs=VMEM,
            scratch_shapes=[pltpu.VMEM((n * chunk, 2 * windows * LANES), BF16)],
            name="products",
            compiler_params=params,
        )(gather, *arrived)

    def more_rounds(ops):
        gather, arrived, found, place, keep, other, most = ops
        data = jnp.concatenate([jnp.concatenate([keep[w], other[w]], axis=1) for w in range(windows)], axis=1)
        taken = dot(gather, jnp.concatenate(arrived))

        def again(state):
            done, taken = state
            new = []
            for k in range(n):
                select = (jnp.arange(chunk, dtype=I32)[:, None] + done == place[k][None, :]).astype(BF16)
                out = dot(select, data).astype(BF16)
                new.append(swap(out, "chan", n, k) if k else out)
            at = found[:, 1:] - done
            slot = jnp.where((at >= 0) & (at < chunk), found[:, :1] * chunk + at, -1)
            pick = (jnp.arange(n * chunk, dtype=I32)[None, :] == slot).astype(BF16)
            return done + chunk, taken + dot(pick, jnp.concatenate(new))

        _, taken = lax.while_loop(lambda state: state[0] < most, again, (jnp.int32(chunk), taken))
        a = taken.reshape(2, pair_count, 2 * windows, 2, LANES // 2)
        a, b = a[0], a[1]
        real = jnp.sum(a[:, :, 0] * b[:, :, 0] + a[:, :, 1] * b[:, :, 1], axis=1)
        imag = jnp.sum(a[:, :, 1] * b[:, :, 0] - a[:, :, 0] * b[:, :, 1], axis=1)
        return jnp.concatenate([real, imag], axis=1).astype(BF16)

    ops = (gather, arrived, found, place, keep, other, most)
    total = lax.cond(most > chunk, more_rounds, one_round, ops)
    bit = 2
    while bit < tm:
        sent = total.astype(BF16)
        total = sent.astype(F32) + swap(sent, "tm", tm, bit).astype(F32)
        bit *= 2
    total = total.astype(F32)
    second = swap(total, "tm", tm, 1)
    return pl.pallas_call(
        functools.partial(finish_kernel, 1.0 / (windows * tm)),
        out_shape=jax.ShapeDtypeStruct((pair_count, 2 * LANES), F32),
        in_specs=[SMEM, VMEM, VMEM],
        out_specs=VMEM,
        name="finish",
        compiler_params=params,
    )(core, total, second)


def solution(mesh):
    tm, n = mesh.shape["tm"], mesh.shape["chan"]
    in_specs = (P("tm", "chan", None), P(), P(), P("chan", None))
    out_specs = P("chan", None)
    return jax.shard_map(
        functools.partial(local, tm, n), mesh=mesh, in_specs=in_specs, out_specs=out_specs, check_vma=False
    )
```

```python
import functools

import jax
import jax.numpy as jnp
import ml_dtypes
import numpy as np
from jax import lax
from jax.experimental import pallas as pl
from jax.experimental.pallas import tpu as pltpu
from jax.sharding import PartitionSpec as P

NB = 128
SMOOTH = 4
LANES = 128
MARK_FLOPS = 2 * 10**10
ROUND_ROWS = 56

F32, BF16, I32 = jnp.float32, jnp.bfloat16, jnp.int32
VMEM = pl.BlockSpec(memory_space=pltpu.VMEM)
SMEM = pl.BlockSpec(memory_space=pltpu.SMEM)
NT = (((1,), (1,)), ((), ()))


def table_of(length, pad):
    samples = np.arange(length, dtype=np.int64)
    freqs = np.arange(1, NB + 1, dtype=np.int64)
    phase = (samples[:, None] * freqs[None, :] % length).astype(np.float32)
    angles = (phase * np.float32(2.0 * np.pi / length)).astype(np.float64)
    table = np.concatenate([np.cos(angles), -np.sin(angles)], axis=1).astype(np.float32)
    table = np.concatenate([table, np.zeros((pad, 2 * NB), np.float32)])
    return table.astype(ml_dtypes.bfloat16)


def dot(a, b, dims=(((1,), (0,)), ((), ()))):
    return lax.dot_general(a, b, dims, preferred_element_type=F32)


def iota(shape, axis):
    return lax.broadcasted_iota(I32, shape, axis)


def spectrum_kernel(core_ref, taps_ref, table_ref, raw_ref, keep_ref, give_ref, rows_ref, mat_ref, sem):
    windows = raw_ref.shape[0]
    copies = [pltpu.make_async_copy(raw_ref.at[w], rows_ref.at[w], sem.at[w]) for w in range(windows)]
    for copy in copies:
        copy.start()
    taps = taps_ref[...].astype(F32)
    n = taps.shape[1]
    wide = jnp.concatenate([taps, jnp.zeros_like(taps)], axis=1)
    toeplitz = pltpu.roll(jnp.broadcast_to(wide, (n, 2 * n)), 0, 1, stride=1, stride_axis=0).astype(BF16)
    for b in range(mat_ref.shape[0] // n):
        mat_ref[b * n : (b + 1) * n, :] = dot(toeplitz, table_ref[b * n : (b + 2) * n, :]).astype(BF16)
    shape = (2 * NB, 2 * NB)
    near = jnp.abs(iota(shape, 0) % NB - iota(shape, 1)) <= SMOOTH
    averaging = jnp.where(near | (iota(shape, 1) >= NB), 1.0, 0.0).astype(BF16)
    bins = iota((1, NB), 1)
    counts = jnp.minimum(bins, SMOOTH) + jnp.minimum(NB - 1 - bins, SMOOTH) + 1
    inverse = 1.0 / counts.astype(F32)
    first_core = core_ref[0] == 0
    half = NB // 2

    def whiten(w, spec):
        re, im = spec[:, :NB], spec[:, NB:]
        mag = jnp.sqrt(re * re + im * im)
        high = mag.astype(BF16)
        low = (mag - high.astype(F32)).astype(BF16)
        sums = dot(jnp.concatenate([high, low], axis=1), averaging)
        divisor = sums[:, :NB] * inverse + sums[:, NB:] * (0.1 / NB) + 1e-06
        scale = 1.0 / divisor
        re = re * scale
        im = im * scale
        left = iota(re.shape, 1) < half
        first = jnp.where(left, re, pltpu.roll(im, half, 1))
        second = jnp.where(left, pltpu.roll(re, half, 1), im)
        keep_ref[w] = jnp.where(first_core, first, second).astype(BF16)
        give_ref[w] = jnp.where(first_core, second, first).astype(BF16)

    for start in range(0, windows, 2):
        pair = range(start, min(start + 2, windows))
        for w in pair:
            copies[w].wait()
        specs = [dot(rows_ref[w], mat_ref[...]) for w in pair]
        for w, spec in zip(pair, specs):
            whiten(w, spec)


def lane_sum(value):
    return jnp.sum(value, axis=1, keepdims=True)


def mark_kernel(high_count, pairs_ref, marks_ref):
    table = None
    for j in range(2):
        ids = pairs_ref[j : j + 1, :]
        high = (iota((high_count, ids.shape[1]), 0) == ids // LANES).astype(F32).astype(BF16)
        low = (iota((LANES, ids.shape[1]), 0) == ids % LANES).astype(F32).astype(BF16)
        part = dot(high, low, NT)
        table = part if table is None else table + part
    bits = jnp.where(table > 0.5, 1, 0) << (iota(table.shape, 0) % 32)
    for w in range(marks_ref.shape[1] // LANES):
        word = bits[32 * w : min(32 * w + 32, high_count), :]
        marks_ref[:, w * LANES : (w + 1) * LANES] = jnp.sum(word, axis=0, keepdims=True)


def wanted(marks, ids):
    parts = []
    words = marks.shape[1] // LANES
    for g in range(ids.shape[1] // LANES):
        here = ids[:, g * LANES : (g + 1) * LANES]
        high, low = here // LANES, here % LANES
        found = jnp.zeros_like(here)
        for w in range(words):
            word = jnp.take_along_axis(marks[:, w * LANES : (w + 1) * LANES], low, axis=1)
            found = jnp.where(high // 32 == w, word, found)
        parts.append((found >> (high % 32)) & 1)
    return parts


def places(parts):
    ahead = (iota((LANES, LANES), 0) < iota((LANES, LANES), 1)).astype(F32).astype(BF16)
    count = None
    out = []
    for part in parts:
        value = part.astype(F32)
        place = dot(value.astype(BF16), ahead)
        if count is not None:
            place = place + count
        out.append(jnp.where(part > 0, place, -1.0).astype(I32))
        total = lane_sum(value)
        count = total if count is None else count + total
    return jnp.concatenate(out, axis=1), count


def spread(row, count):
    return jnp.broadcast_to(row, (count, row.shape[1]))


def stacked(refs):
    marks = jnp.concatenate([ref[...] for ref in refs], axis=0)
    pad = -marks.shape[0] % 8
    if pad:
        marks = jnp.concatenate([marks, jnp.zeros((pad, marks.shape[1]), I32)], axis=0)
    return marks


def pack_kernel(lines, pieces, me_ref, *refs):
    marks = stacked(refs[:pieces])
    chan_ref, keep_ref, other_ref = refs[pieces : pieces + 3]
    chunk_refs = refs[pieces + 3 :]
    chunk = chunk_refs[0].shape[0]
    rows = chan_ref.shape[1]
    ids = spread(chan_ref[pl.ds(me_ref[0], 1), :], marks.shape[0])
    place, _ = places(wanted(marks, ids))
    slots = iota((chunk, rows), 0)
    select = [(slots == place[i : i + 1, :]).astype(F32).astype(BF16) for i in lines]
    select = jnp.concatenate(select, axis=0)
    for w in range(keep_ref.shape[0]):
        data = jnp.concatenate([keep_ref[w], other_ref[w]], axis=1)
        out = dot(select, data).astype(BF16)
        for i in range(len(lines)):
            chunk_refs[i][:, 2 * w * LANES : 2 * (w + 1) * LANES] = out[i * chunk : (i + 1) * chunk]


def arrival_kernel(sources, chunk, pieces, me_ref, *refs):
    marks = stacked(refs[:pieces])
    chan_ref, pairs_ref, early_ref, late_ref, most_ref = refs[pieces:]
    n = len(sources)
    ids = jnp.concatenate([chan_ref[pl.ds(me_ref[0] ^ k, 1), :] for k in sources], axis=0)
    most = None
    for k in range(n):
        parts = wanted(spread(marks[k : k + 1, :], n), ids)
        if k == 0:
            place, count = places(parts)
        else:
            count = lane_sum(sum(parts).astype(F32))
        most = count if most is None else jnp.maximum(most, count)
    most_ref[...] = jnp.max(most, axis=0, keepdims=True).astype(I32)
    slots = iota((chunk, ids.shape[1]), 0)
    here = []
    for s in range(n):
        held = jnp.where(slots == place[s : s + 1, :], ids[s : s + 1, :] + 1, 0)
        here.append(lane_sum(held.astype(F32)))
    column = jnp.concatenate(here, axis=0) - 1.0
    row = jnp.broadcast_to(column, (n * chunk, LANES)).T[:1, :]
    ends = pairs_ref[...].astype(F32)
    count = ends.shape[1]
    ends = jnp.concatenate([ends, jnp.zeros((6, count), F32)], axis=0).T
    middle = n // 2 * chunk
    for j in range(2):
        match = ends[:, j : j + 1] == row
        match = jnp.where(match, 1.0, 0.0).astype(BF16)
        early_ref[j * count : (j + 1) * count, :] = match[:, :middle]
        late_ref[j * count : (j + 1) * count, :] = match[:, middle:]


def early_kernel(half, gather_ref, *refs):
    chunk_refs, out_ref, rows_ref = refs[:half], refs[half], refs[half + 1]
    chunk = chunk_refs[0].shape[0]
    for k in range(half):
        rows_ref[k * chunk : (k + 1) * chunk, :] = chunk_refs[k][...]
    for w in range(0, rows_ref.shape[1], 2 * LANES):
        out_ref[:, w : w + 2 * LANES] = dot(gather_ref[...], rows_ref[:, w : w + 2 * LANES]).astype(BF16)


def product_kernel(half, start, early_ref, gather_ref, *refs):
    chunk_refs, out_ref, rows_ref = refs[:half], refs[half], refs[half + 1]
    chunk = chunk_refs[0].shape[0]
    for k in range(half):
        rows_ref[k * chunk : (k + 1) * chunk, :] = chunk_refs[k][...]
    count = out_ref.shape[0]
    total = gather_ref.shape[0] // 2
    pick = jnp.concatenate([gather_ref[start : start + count, :], gather_ref[total + start : total + start + count, :]])
    middle = LANES // 2
    straight = crossed = None
    for w in range(0, rows_ref.shape[1] // LANES, 2):
        ends = dot(pick, rows_ref[:, w * LANES : (w + 2) * LANES])
        for v in range(2):
            lanes = slice((w + v) * LANES, (w + v + 1) * LANES)
            a = ends[:count, v * LANES : (v + 1) * LANES] + early_ref[start : start + count, lanes].astype(F32)
            b = ends[count:, v * LANES : (v + 1) * LANES] + early_ref[total + start : total + start + count, lanes].astype(F32)
            turned = pltpu.roll(a, middle, 1)
            straight = a * b if straight is None else straight + a * b
            crossed = turned * b if crossed is None else crossed + turned * b
    real = straight + pltpu.roll(straight, middle, 1)
    imag = pltpu.roll(crossed, middle, 1) - crossed
    out_ref[...] = jnp.where(iota(real.shape, 1) < middle, real, imag).astype(out_ref.dtype)


def finish_kernel(factor, core_ref, *refs):
    parts = (len(refs) - 1) // 2
    out_ref = refs[-1]
    first_core = core_ref[0] == 0
    half = LANES // 2
    start = 0
    for i in range(parts):
        mine = refs[i][...] * factor
        other = refs[parts + i][...] * factor
        first = jnp.where(first_core, mine, other)
        second = jnp.where(first_core, other, mine)
        left = iota(first.shape, 1) < half
        here = slice(start, start + first.shape[0])
        start += first.shape[0]
        out_ref[here, :LANES] = jnp.where(left, first, pltpu.roll(second, half, 1))
        out_ref[here, LANES:] = jnp.where(left, pltpu.roll(first, half, 1), second)


def swap(value, axis, size, bit):
    return lax.ppermute(value, axis, [(i, i ^ bit) for i in range(size)])


def call(kernel, out, flops=0, scratch=(), smem=1):
    def run(*args):
        many = isinstance(out, (tuple, list))
        specs = [SMEM] * smem + [VMEM] * (len(args) - smem)
        outs = list(out) if many else [out]
        size = sum(a.size * a.dtype.itemsize for a in args) + sum(o.size * o.dtype.itemsize for o in outs)
        return pl.pallas_call(
            kernel,
            out_shape=tuple(out) if many else out,
            in_specs=specs,
            out_specs=(VMEM,) * len(outs) if many else VMEM,
            scratch_shapes=scratch,
            compiler_params=pltpu.CompilerParams(vmem_limit_bytes=24 * 1024 * 1024),
            cost_estimate=pl.CostEstimate(flops=flops, bytes_accessed=size, transcendentals=0),
        )(*args)

    return run


def spectra(tm, core, raw_blocks, fir_taps):
    windows, rows, length = raw_blocks.shape
    table = jnp.asarray(table_of(length, fir_taps.shape[0]))
    half = jax.ShapeDtypeStruct((windows, rows, NB), BF16)
    keep, give = pl.pallas_call(
        spectrum_kernel,
        out_shape=(half, half),
        in_specs=[SMEM, VMEM, VMEM, pl.BlockSpec(memory_space=pl.ANY)],
        out_specs=(VMEM, VMEM),
        scratch_shapes=[
            pltpu.VMEM(raw_blocks.shape, BF16),
            pltpu.VMEM((length, 2 * NB), BF16),
            pltpu.SemaphoreType.DMA((windows,)),
        ],
        compiler_params=pltpu.CompilerParams(vmem_limit_bytes=24 * 1024 * 1024),
        cost_estimate=pl.CostEstimate(
            flops=2 * windows * rows * length * 2 * NB, bytes_accessed=2 * windows * rows * length, transcendentals=0
        ),
    )(core, fir_taps.reshape(1, -1), table, raw_blocks)
    return keep, swap(give, "tm", tm, 1)


def all_rounds(tm, n, chunk, order, me, core, raw_blocks, fir_taps, by_block, pairs, marks, most):
    windows, rows, _ = raw_blocks.shape
    pair_count = pairs.shape[0]
    width = 2 * windows * LANES
    data = jnp.concatenate(spectra(tm, core, raw_blocks, fir_taps), axis=0)
    data = data.transpose(1, 0, 2).reshape(rows, width)
    marks = jnp.concatenate(marks)

    def is_marked(words, ids):
        word = words.reshape(-1)[(ids // LANES // 32) * LANES + ids % LANES]
        return (word >> (ids // LANES % 32)) & 1

    mine = by_block[me[0]]
    want = jnp.stack([is_marked(marks[order.index(k)], mine) for k in range(n)])
    place = jnp.where(want > 0, jnp.cumsum(want, axis=1) - 1, -1)
    held = is_marked(marks[0], by_block)
    rank = jnp.cumsum(held, axis=1) - 1
    relative = jnp.arange(n, dtype=I32) ^ me[0]
    counts = jnp.sum(held, axis=1)[relative]
    offsets = jnp.cumsum(counts) - counts
    line_of_row = (offsets[relative][:, None] + rank).reshape(-1)
    ends = pairs.T.reshape(-1)
    line = jnp.sum(jnp.where(ends[:, None] == by_block.reshape(1, -1), line_of_row[None, :], 0), axis=1)
    lines = jnp.arange(n * chunk, dtype=I32)

    def again(inner):
        done, merged = inner
        slot = jnp.arange(chunk, dtype=I32) + done
        select = (slot[None, :, None] == place[:, None, :]).astype(BF16).reshape(n * chunk, rows)
        packed = dot(select, data).astype(BF16)
        new = [packed[k * chunk : (k + 1) * chunk] for k in range(n)]
        new = jnp.concatenate([swap(new[k], "chan", n, k) if k else new[k] for k in range(n)])
        target = jnp.where(slot[None, :] < counts[:, None], offsets[:, None] + slot[None, :], -1).reshape(1, -1)
        return done + chunk, merged + dot((lines[:, None] == target).astype(BF16), new).astype(BF16)

    start = (jnp.int32(0), jnp.zeros((n * chunk, width), BF16))
    _, merged = lax.while_loop(lambda inner: inner[0] < most[0, 0], again, start)
    taken = dot((lines[None, :] == line[:, None]).astype(BF16), merged)
    taken = taken.reshape(2, pair_count, 2 * windows, 2, LANES // 2)
    a, b = taken[0], taken[1]
    real = jnp.sum(a[:, :, 0] * b[:, :, 0] + a[:, :, 1] * b[:, :, 1], axis=1)
    imag = jnp.sum(a[:, :, 1] * b[:, :, 0] - a[:, :, 0] * b[:, :, 1], axis=1)
    total = jnp.concatenate([real, imag], axis=1)
    bit = 2
    while bit < tm:
        total = total + swap(total, "tm", tm, bit)
        bit *= 2
    return finish(core, tm, windows, [total], [swap(total, "tm", tm, 1)])


def finish(core, tm, windows, mine, other):
    rows = sum(value.shape[0] for value in mine)
    kernel = functools.partial(finish_kernel, 1.0 / (windows * tm))
    return call(kernel, jax.ShapeDtypeStruct((rows, 2 * LANES), F32))(core, *mine, *other)


def steps_of(n):
    bits = [n // 2] + [1 << i for i in range(n.bit_length() - 2)]
    order, known = [0], []
    for bit in bits:
        known.append([k ^ bit for k in order])
        order = order + known[-1]
    return bits, known, order


def arrivals(n):
    _, known, _ = steps_of(n)
    sends = [k for ks in known for k in sorted(ks) if k >= n // 2] + list(range(n // 2 - 1, 0, -1))
    return sends, [0] + sends[: n // 2 - 1], sends[n // 2 - 1 :]


def local(tm, n, raw_blocks, fir_taps, recorder_channel, pairs):
    windows, rows, _ = raw_blocks.shape
    pair_count = pairs.shape[0]
    chunk = ROUND_ROWS
    half = n // 2
    high_count = n * rows // LANES
    shaped = jax.ShapeDtypeStruct
    me = lax.axis_index("chan").astype(I32).reshape(1)
    core = (lax.axis_index("tm") % 2).astype(I32).reshape(1)
    by_block = recorder_channel.reshape(n, rows)
    width = 2 * windows * LANES
    bits, known, order = steps_of(n)
    _, early, late = arrivals(n)

    mark_shape = shaped((1, -(-high_count // 32) * LANES), I32)
    own = call(functools.partial(mark_kernel, high_count), mark_shape, flops=MARK_FLOPS, smem=0)(pairs.T)
    keep, other = spectra(tm, core, raw_blocks, fir_taps)

    marks = [own]
    arrived = [None] * n
    for i, bit in enumerate(bits):
        new = swap(jnp.concatenate(marks), "chan", n, bit)
        here = [new] if i else [new, own]
        marks.append(new)
        owners = known[i] if i else known[i] + [0]
        kernel = functools.partial(pack_kernel, list(range(len(owners))), len(here))
        packed = call(kernel, [shaped((chunk, width), BF16)] * len(owners))(me, *here, by_block, keep, other)
        for k, value in zip(owners, packed):
            arrived[k] = swap(value, "chan", n, k) if k else value

    shapes = [shaped((2 * pair_count, half * chunk), BF16)] * 2 + [shaped((1, 1), I32)]
    kernel = functools.partial(arrival_kernel, early + late, chunk, len(marks))
    pick_early, pick_late, most = call(kernel, shapes)(me, *marks, by_block, pairs.T)
    scratch = [pltpu.VMEM((half * chunk, width), BF16)]
    found = call(
        functools.partial(early_kernel, half),
        shaped((2 * pair_count, width), BF16),
        flops=4 * pair_count * half * chunk * width,
        scratch=scratch,
        smem=0,
    )(pick_early, *[arrived[k] for k in early])

    sizes = [pair_count * 3 // 4, pair_count // 4]
    totals, seconds = [], []
    for i, size in enumerate(sizes):
        total = call(
            functools.partial(product_kernel, half, sum(sizes[:i])),
            shaped((size, LANES), BF16),
            flops=4 * size * half * chunk * width,
            scratch=scratch,
            smem=0,
        )(found, pick_late, *[arrived[k] for k in late])
        bit = 2
        while bit < tm:
            sent = total.astype(BF16)
            total = sent.astype(F32) + swap(sent, "tm", tm, bit).astype(F32)
            bit *= 2
        totals.append(total.astype(F32))
    for total in totals:
        seconds.append(swap(total, "tm", tm, 1))
    result = finish(core, tm, windows, totals, seconds)

    def rounds(state):
        given = lax.optimization_barrier((state[0], me, core, raw_blocks, fir_taps, by_block, pairs, marks, most))
        return jnp.int32(0), all_rounds(tm, n, chunk, order, *given[1:])

    more = jnp.where(most[0, 0] > chunk, 1, 0)
    return lax.while_loop(lambda state: state[0] > 0, rounds, (more, result))[1]


def solution(mesh):
    tm, n = mesh.shape["tm"], mesh.shape["chan"]
    in_specs = (P("tm", "chan", None), P(), P(), P("chan", None))
    out_specs = P("chan", None)

    def body(*args):
        return local(tm, n, *args)

    return jax.shard_map(body, mesh=mesh, in_specs=in_specs, out_specs=out_specs, check_vma=False)
```

```python
import functools

import jax
import jax.numpy as jnp
import ml_dtypes
import numpy as np
from jax import lax
from jax.experimental import pallas as pl
from jax.experimental.pallas import tpu as pltpu
from jax.sharding import PartitionSpec as P

NB = 128
SMOOTH = 4
LANES = 128
FIRST_FLOPS = 2 * 10**10
SENDS = [4, 1, 5, 2, 6, 3, 7]
EARLY = [0, 4, 1, 5]
ROUND_ROWS = 56

F32, BF16, I32 = jnp.float32, jnp.bfloat16, jnp.int32
VMEM = pl.BlockSpec(memory_space=pltpu.VMEM)
SMEM = pl.BlockSpec(memory_space=pltpu.SMEM)
NT = (((1,), (1,)), ((), ()))


def table_of(length, pad):
    samples = np.arange(length, dtype=np.int64)
    freqs = np.arange(1, NB + 1, dtype=np.int64)
    phase = (samples[:, None] * freqs[None, :] % length).astype(np.float32)
    angles = (phase * np.float32(2.0 * np.pi / length)).astype(np.float64)
    table = np.concatenate([np.cos(angles), -np.sin(angles)], axis=1).astype(np.float32)
    table = np.concatenate([table, np.zeros((pad, 2 * NB), np.float32)])
    return table.astype(ml_dtypes.bfloat16)


def dot(a, b, dims=(((1,), (0,)), ((), ()))):
    return lax.dot_general(a, b, dims, preferred_element_type=F32)


def iota(shape, axis):
    return lax.broadcasted_iota(I32, shape, axis)


def averaging_kernel(core_ref, out_ref):
    shape = out_ref.shape
    near = jnp.abs(iota(shape, 0) % NB - iota(shape, 1)) <= SMOOTH
    out_ref[...] = jnp.where(near | (iota(shape, 1) >= NB), 1.0, 0.0).astype(BF16)


def spectrum_kernel(core_ref, taps_ref, table_ref, sum_ref, raw_ref, keep_ref, give_ref, rows_ref, mat_ref, sem):
    windows = raw_ref.shape[0]
    copies = [pltpu.make_async_copy(raw_ref.at[w], rows_ref.at[w], sem.at[w]) for w in range(windows)]
    for copy in copies:
        copy.start()
    taps = taps_ref[...].astype(F32)
    n = taps.shape[1]
    wide = jnp.concatenate([taps, jnp.zeros_like(taps)], axis=1)
    toeplitz = pltpu.roll(jnp.broadcast_to(wide, (n, 2 * n)), 0, 1, stride=1, stride_axis=0).astype(BF16)
    for b in range(mat_ref.shape[0] // n):
        mat_ref[b * n : (b + 1) * n, :] = dot(toeplitz, table_ref[b * n : (b + 2) * n, :]).astype(BF16)
    averaging = sum_ref[...]
    bins = iota((1, NB), 1)
    counts = jnp.minimum(bins, SMOOTH) + jnp.minimum(NB - 1 - bins, SMOOTH) + 1
    inverse = 1.0 / counts.astype(F32)
    first_core = core_ref[0] == 0
    half = NB // 2

    def whiten(w, spec):
        re, im = spec[:, :NB], spec[:, NB:]
        mag = jnp.sqrt(re * re + im * im)
        high = mag.astype(BF16)
        low = (mag - high.astype(F32)).astype(BF16)
        sums = dot(jnp.concatenate([high, low], axis=1), averaging)
        divisor = sums[:, :NB] * inverse + sums[:, NB:] * (0.1 / NB) + 1e-06
        scale = 1.0 / divisor
        re = re * scale
        im = im * scale
        left = iota(re.shape, 1) < half
        first = jnp.where(left, re, pltpu.roll(im, half, 1))
        second = jnp.where(left, pltpu.roll(re, half, 1), im)
        keep_ref[w] = jnp.where(first_core, first, second).astype(BF16)
        give_ref[w] = jnp.where(first_core, second, first).astype(BF16)

    for start in range(0, windows, 2):
        pair = range(start, min(start + 2, windows))
        for w in pair:
            copies[w].wait()
        specs = [dot(rows_ref[w], mat_ref[...]) for w in pair]
        for w, spec in zip(pair, specs):
            whiten(w, spec)


def lane_sum(value):
    return jnp.sum(value, axis=1, keepdims=True)


def mark_kernel(high_count, *refs):
    for pairs_ref, marks_ref in zip(refs[: len(refs) // 2], refs[len(refs) // 2 :]):
        mark(high_count, pairs_ref, marks_ref)


def mark(high_count, pairs_ref, marks_ref):
    table = None
    for j in range(2):
        ids = pairs_ref[j : j + 1, :]
        high = (iota((high_count, ids.shape[1]), 0) == ids // LANES).astype(F32).astype(BF16)
        low = (iota((LANES, ids.shape[1]), 0) == ids % LANES).astype(F32).astype(BF16)
        part = dot(high, low, NT)
        table = part if table is None else table + part
    bits = jnp.where(table > 0.5, 1, 0) << (iota(table.shape, 0) % 32)
    for w in range(marks_ref.shape[1] // LANES):
        word = bits[32 * w : min(32 * w + 32, high_count), :]
        marks_ref[:, w * LANES : (w + 1) * LANES] = jnp.sum(word, axis=0, keepdims=True)


def wanted(marks, ids):
    parts = []
    words = marks.shape[1] // LANES
    for g in range(ids.shape[1] // LANES):
        here = ids[:, g * LANES : (g + 1) * LANES]
        high, low = here // LANES, here % LANES
        found = jnp.zeros_like(here)
        for w in range(words):
            word = jnp.take_along_axis(marks[:, w * LANES : (w + 1) * LANES], low, axis=1)
            found = jnp.where(high // 32 == w, word, found)
        parts.append((found >> (high % 32)) & 1)
    return parts


def places(parts):
    ahead = (iota((LANES, LANES), 0) < iota((LANES, LANES), 1)).astype(F32).astype(BF16)
    count = None
    out = []
    for part in parts:
        value = part.astype(F32)
        place = dot(value.astype(BF16), ahead)
        if count is not None:
            place = place + count
        out.append(jnp.where(part > 0, place, -1.0).astype(I32))
        total = lane_sum(value)
        count = total if count is None else count + total
    return jnp.concatenate(out, axis=1), count


def spread(row, count):
    return jnp.broadcast_to(row, (count, row.shape[1]))


def stacked(refs):
    marks = jnp.concatenate([ref[...] for ref in refs], axis=0)
    pad = -marks.shape[0] % 8
    if pad:
        marks = jnp.concatenate([marks, jnp.zeros((pad, marks.shape[1]), I32)], axis=0)
    return marks


def pack_kernel(lines, pieces, me_ref, *refs):
    marks = stacked(refs[:pieces])
    chan_ref, keep_ref, other_ref = refs[pieces : pieces + 3]
    chunk_refs = refs[pieces + 3 :]
    chunk = chunk_refs[0].shape[0]
    rows = chan_ref.shape[1]
    ids = spread(chan_ref[pl.ds(me_ref[0], 1), :], marks.shape[0])
    place, _ = places(wanted(marks, ids))
    slots = iota((chunk, rows), 0)
    select = [(slots == place[i : i + 1, :]).astype(F32).astype(BF16) for i in lines]
    select = jnp.concatenate(select, axis=0)
    for w in range(keep_ref.shape[0]):
        data = jnp.concatenate([keep_ref[w], other_ref[w]], axis=1)
        out = dot(select, data).astype(BF16)
        for i in range(len(lines)):
            chunk_refs[i][:, 2 * w * LANES : 2 * (w + 1) * LANES] = out[i * chunk : (i + 1) * chunk]


def arrival_kernel(sources, chunk, pieces, me_ref, *refs):
    marks = stacked(refs[:pieces])
    chan_ref, pairs_ref, early_ref, late_ref, most_ref = refs[pieces:]
    n = len(sources)
    ids = jnp.concatenate([chan_ref[pl.ds(me_ref[0] ^ k, 1), :] for k in sources], axis=0)
    most = None
    for k in range(n):
        parts = wanted(spread(marks[k : k + 1, :], n), ids)
        if k == 0:
            place, count = places(parts)
        else:
            count = lane_sum(sum(parts).astype(F32))
        most = count if most is None else jnp.maximum(most, count)
    most_ref[...] = jnp.max(most, axis=0, keepdims=True).astype(I32)
    slots = iota((chunk, ids.shape[1]), 0)
    here = []
    for s in range(n):
        held = jnp.where(slots == place[s : s + 1, :], ids[s : s + 1, :] + 1, 0)
        here.append(lane_sum(held.astype(F32)))
    column = jnp.concatenate(here, axis=0) - 1.0
    row = jnp.broadcast_to(column, (n * chunk, LANES)).T[:1, :]
    ends = pairs_ref[...].astype(F32)
    count = ends.shape[1]
    ends = jnp.concatenate([ends, jnp.zeros((6, count), F32)], axis=0).T
    middle = n // 2 * chunk
    for j in range(2):
        match = ends[:, j : j + 1] == row
        match = jnp.where(match, 1.0, 0.0).astype(BF16)
        early_ref[j * count : (j + 1) * count, :] = match[:, :middle]
        late_ref[j * count : (j + 1) * count, :] = match[:, middle:]


def early_kernel(half, gather_ref, *refs):
    chunk_refs, out_ref, rows_ref = refs[:half], refs[half], refs[half + 1]
    chunk = chunk_refs[0].shape[0]
    for k in range(half):
        rows_ref[k * chunk : (k + 1) * chunk, :] = chunk_refs[k][...]
    for w in range(0, rows_ref.shape[1], 2 * LANES):
        out_ref[:, w : w + 2 * LANES] = dot(gather_ref[...], rows_ref[:, w : w + 2 * LANES]).astype(BF16)


def product_kernel(half, start, early_ref, gather_ref, *refs):
    chunk_refs, out_ref, rows_ref = refs[:half], refs[half], refs[half + 1]
    chunk = chunk_refs[0].shape[0]
    for k in range(half):
        rows_ref[k * chunk : (k + 1) * chunk, :] = chunk_refs[k][...]
    count = out_ref.shape[0]
    total = gather_ref.shape[0] // 2
    pick = jnp.concatenate([gather_ref[start : start + count, :], gather_ref[total + start : total + start + count, :]])
    middle = LANES // 2
    straight = crossed = None
    for w in range(0, rows_ref.shape[1] // LANES, 2):
        ends = dot(pick, rows_ref[:, w * LANES : (w + 2) * LANES])
        for v in range(2):
            lanes = slice((w + v) * LANES, (w + v + 1) * LANES)
            a = ends[:count, v * LANES : (v + 1) * LANES] + early_ref[start : start + count, lanes].astype(F32)
            b = ends[count:, v * LANES : (v + 1) * LANES] + early_ref[total + start : total + start + count, lanes].astype(F32)
            turned = pltpu.roll(a, middle, 1)
            straight = a * b if straight is None else straight + a * b
            crossed = turned * b if crossed is None else crossed + turned * b
    real = straight + pltpu.roll(straight, middle, 1)
    imag = pltpu.roll(crossed, middle, 1) - crossed
    out_ref[...] = jnp.where(iota(real.shape, 1) < middle, real, imag).astype(out_ref.dtype)


def finish_kernel(factor, core_ref, *refs):
    parts = (len(refs) - 1) // 2
    out_ref = refs[-1]
    first_core = core_ref[0] == 0
    half = LANES // 2
    start = 0
    for i in range(parts):
        mine = refs[i][...] * factor
        other = refs[parts + i][...] * factor
        first = jnp.where(first_core, mine, other)
        second = jnp.where(first_core, other, mine)
        left = iota(first.shape, 1) < half
        here = slice(start, start + first.shape[0])
        start += first.shape[0]
        out_ref[here, :LANES] = jnp.where(left, first, pltpu.roll(second, half, 1))
        out_ref[here, LANES:] = jnp.where(left, pltpu.roll(first, half, 1), second)


def swap(value, axis, size, bit):
    return lax.ppermute(value, axis, [(i, i ^ bit) for i in range(size)])


def call(kernel, out, flops=0, scratch=(), smem=1):
    def run(*args):
        many = isinstance(out, (tuple, list))
        specs = [SMEM] * smem + [VMEM] * (len(args) - smem)
        outs = list(out) if many else [out]
        size = sum(a.size * a.dtype.itemsize for a in args) + sum(o.size * o.dtype.itemsize for o in outs)
        return pl.pallas_call(
            kernel,
            out_shape=tuple(out) if many else out,
            in_specs=specs,
            out_specs=(VMEM,) * len(outs) if many else VMEM,
            scratch_shapes=scratch,
            compiler_params=pltpu.CompilerParams(vmem_limit_bytes=24 * 1024 * 1024),
            cost_estimate=pl.CostEstimate(flops=flops, bytes_accessed=size, transcendentals=0),
        )(*args)

    return run


def spectra(tm, core, raw_blocks, fir_taps):
    windows, rows, length = raw_blocks.shape
    table = jnp.asarray(table_of(length, fir_taps.shape[0]))
    shape = jax.ShapeDtypeStruct((2 * NB, 2 * NB), BF16)
    averaging = call(averaging_kernel, shape, flops=FIRST_FLOPS)(core)
    half = jax.ShapeDtypeStruct((windows, rows, NB), BF16)
    keep, give = pl.pallas_call(
        spectrum_kernel,
        out_shape=(half, half),
        in_specs=[SMEM, VMEM, VMEM, VMEM, pl.BlockSpec(memory_space=pl.ANY)],
        out_specs=(VMEM, VMEM),
        scratch_shapes=[
            pltpu.VMEM(raw_blocks.shape, BF16),
            pltpu.VMEM((length, 2 * NB), BF16),
            pltpu.SemaphoreType.DMA((windows,)),
        ],
        compiler_params=pltpu.CompilerParams(vmem_limit_bytes=24 * 1024 * 1024),
        cost_estimate=pl.CostEstimate(
            flops=2 * windows * rows * length * 2 * NB, bytes_accessed=2 * windows * rows * length, transcendentals=0
        ),
    )(core, fir_taps.reshape(1, -1), table, averaging, raw_blocks)
    return keep, swap(give, "tm", tm, 1)


def all_rounds(tm, n, chunk, order, me, core, raw_blocks, fir_taps, by_block, pairs, marks, most):
    windows, rows, _ = raw_blocks.shape
    pair_count = pairs.shape[0]
    width = 2 * windows * LANES
    data = jnp.concatenate(spectra(tm, core, raw_blocks, fir_taps), axis=0)
    data = data.transpose(1, 0, 2).reshape(rows, width)
    marks = jnp.concatenate(marks)

    def is_marked(words, ids):
        word = words.reshape(-1)[(ids // LANES // 32) * LANES + ids % LANES]
        return (word >> (ids // LANES % 32)) & 1

    mine = by_block[me[0]]
    want = jnp.stack([is_marked(marks[order.index(k)], mine) for k in range(n)])
    place = jnp.where(want > 0, jnp.cumsum(want, axis=1) - 1, -1)
    held = is_marked(marks[0], by_block)
    rank = jnp.cumsum(held, axis=1) - 1
    relative = jnp.arange(n, dtype=I32) ^ me[0]
    counts = jnp.sum(held, axis=1)[relative]
    offsets = jnp.cumsum(counts) - counts
    line_of_row = (offsets[relative][:, None] + rank).reshape(-1)
    ends = pairs.T.reshape(-1)
    line = jnp.sum(jnp.where(ends[:, None] == by_block.reshape(1, -1), line_of_row[None, :], 0), axis=1)
    lines = jnp.arange(n * chunk, dtype=I32)

    def again(inner):
        done, merged = inner
        slot = jnp.arange(chunk, dtype=I32) + done
        select = (slot[None, :, None] == place[:, None, :]).astype(BF16).reshape(n * chunk, rows)
        packed = dot(select, data).astype(BF16)
        new = [packed[k * chunk : (k + 1) * chunk] for k in range(n)]
        new = jnp.concatenate([swap(new[k], "chan", n, k) if k else new[k] for k in range(n)])
        target = jnp.where(slot[None, :] < counts[:, None], offsets[:, None] + slot[None, :], -1).reshape(1, -1)
        return done + chunk, merged + dot((lines[:, None] == target).astype(BF16), new).astype(BF16)

    start = (jnp.int32(0), jnp.zeros((n * chunk, width), BF16))
    _, merged = lax.while_loop(lambda inner: inner[0] < most[0, 0], again, start)
    taken = dot((lines[None, :] == line[:, None]).astype(BF16), merged)
    taken = taken.reshape(2, pair_count, 2 * windows, 2, LANES // 2)
    a, b = taken[0], taken[1]
    real = jnp.sum(a[:, :, 0] * b[:, :, 0] + a[:, :, 1] * b[:, :, 1], axis=1)
    imag = jnp.sum(a[:, :, 1] * b[:, :, 0] - a[:, :, 0] * b[:, :, 1], axis=1)
    total = jnp.concatenate([real, imag], axis=1)
    bit = 2
    while bit < tm:
        total = total + swap(total, "tm", tm, bit)
        bit *= 2
    return finish(core, tm, windows, [total], [swap(total, "tm", tm, 1)])


def finish(core, tm, windows, mine, other):
    rows = sum(value.shape[0] for value in mine)
    kernel = functools.partial(finish_kernel, 1.0 / (windows * tm))
    return call(kernel, jax.ShapeDtypeStruct((rows, 2 * LANES), F32))(core, *mine, *other)


def steps_of(n):
    bits = [n // 2] + [1 << i for i in range(n.bit_length() - 2)]
    order, known = [0], []
    for bit in bits:
        known.append([k ^ bit for k in order])
        order = order + known[-1]
    return bits, known, order


def arrivals(n):
    _, known, _ = steps_of(n)
    far = [k for ks in known for k in sorted(ks) if k >= n // 2]
    near = list(range(n // 2 - 1, 0, -1))
    sends = SENDS if n == 8 else far[:-1] + near + far[-1:]
    early = EARLY if n == 8 else [0] + sends[: n // 2 - 1]
    return sends, early, [k for k in sends if k not in early]


def local(tm, n, raw_blocks, fir_taps, recorder_channel, pairs):
    windows, rows, _ = raw_blocks.shape
    pair_count = pairs.shape[0]
    chunk = ROUND_ROWS
    half = n // 2
    high_count = n * rows // LANES
    shaped = jax.ShapeDtypeStruct
    me = lax.axis_index("chan").astype(I32).reshape(1)
    core = (lax.axis_index("tm") % 2).astype(I32).reshape(1)
    by_block = recorder_channel.reshape(n, rows)
    width = 2 * windows * LANES
    bits, known, order = steps_of(n)
    _, early, late = arrivals(n)

    mark_shape = shaped((1, -(-high_count // 32) * LANES), I32)
    keep, other = spectra(tm, core, raw_blocks, fir_taps)
    theirs = swap(pairs.T, "chan", n, bits[0])
    own, new = call(functools.partial(mark_kernel, high_count), [mark_shape] * 2, smem=0)(pairs.T, theirs)

    marks = [own]
    arrived = [None] * n
    for i, bit in enumerate(bits):
        if i:
            new = swap(jnp.concatenate(marks), "chan", n, bit)
        here = [new] if i else [new, own]
        marks.append(new)
        owners = known[i] if i else known[i] + [0]
        kernel = functools.partial(pack_kernel, list(range(len(owners))), len(here))
        packed = call(kernel, [shaped((chunk, width), BF16)] * len(owners))(me, *here, by_block, keep, other)
        for k, value in zip(owners, packed):
            arrived[k] = swap(value, "chan", n, k) if k else value

    shapes = [shaped((2 * pair_count, half * chunk), BF16)] * 2 + [shaped((1, 1), I32)]
    kernel = functools.partial(arrival_kernel, early + late, chunk, len(marks))
    pick_early, pick_late, most = call(kernel, shapes)(me, *marks, by_block, pairs.T)
    scratch = [pltpu.VMEM((half * chunk, width), BF16)]
    found = call(
        functools.partial(early_kernel, half),
        shaped((2 * pair_count, width), BF16),
        flops=4 * pair_count * half * chunk * width,
        scratch=scratch,
        smem=0,
    )(pick_early, *[arrived[k] for k in early])

    sizes = [pair_count * 5 // 8, pair_count * 3 // 8]
    totals, seconds = [], []
    for i, size in enumerate(sizes):
        total = call(
            functools.partial(product_kernel, half, sum(sizes[:i])),
            shaped((size, LANES), BF16),
            flops=4 * size * half * chunk * width,
            scratch=scratch,
            smem=0,
        )(found, pick_late, *[arrived[k] for k in late])
        bit = 2
        while bit < tm:
            sent = total.astype(BF16)
            total = sent.astype(F32) + swap(sent, "tm", tm, bit).astype(F32)
            bit *= 2
        totals.append(total.astype(F32))
    for total in totals:
        seconds.append(swap(total, "tm", tm, 1))
    result = finish(core, tm, windows, totals, seconds)

    def rounds(state):
        given = lax.optimization_barrier((state[0], me, core, raw_blocks, fir_taps, by_block, pairs, marks, most))
        return jnp.int32(0), all_rounds(tm, n, chunk, order, *given[1:])

    more = jnp.where(most[0, 0] > chunk, 1, 0)
    return lax.while_loop(lambda state: state[0] > 0, rounds, (more, result))[1]


def solution(mesh):
    tm, n = mesh.shape["tm"], mesh.shape["chan"]
    in_specs = (P("tm", "chan", None), P(), P(), P("chan", None))
    out_specs = P("chan", None)

    def body(*args):
        return local(tm, n, *args)

    return jax.shard_map(body, mesh=mesh, in_specs=in_specs, out_specs=out_specs, check_vma=False)
```

```python
import functools

import jax
import jax.numpy as jnp
import ml_dtypes
import numpy as np
from jax import lax
from jax.experimental import pallas as pl
from jax.experimental.pallas import tpu as pltpu
from jax.sharding import PartitionSpec as P

NB = 128
SMOOTH = 4
LANES = 128
FIRST_FLOPS = 2 * 10**10
SENDS = [4, 1, 5, 2, 3, 6, 7]
EARLY = [0, 4, 1, 5]
ROUND_ROWS = 52

F32, BF16, I32 = jnp.float32, jnp.bfloat16, jnp.int32
VMEM = pl.BlockSpec(memory_space=pltpu.VMEM)
SMEM = pl.BlockSpec(memory_space=pltpu.SMEM)
NT = (((1,), (1,)), ((), ()))


def table_of(length, pad):
    samples = np.arange(length, dtype=np.int64)
    freqs = np.arange(1, NB + 1, dtype=np.int64)
    phase = (samples[:, None] * freqs[None, :] % length).astype(np.float32)
    angles = (phase * np.float32(2.0 * np.pi / length)).astype(np.float64)
    table = np.concatenate([np.cos(angles), -np.sin(angles)], axis=1).astype(np.float32)
    table = np.concatenate([table, np.zeros((pad, 2 * NB), np.float32)])
    return table.astype(ml_dtypes.bfloat16)


def dot(a, b, dims=(((1,), (0,)), ((), ()))):
    return lax.dot_general(a, b, dims, preferred_element_type=F32)


def iota(shape, axis):
    return lax.broadcasted_iota(I32, shape, axis)


def averaging_kernel(core_ref, out_ref):
    shape = out_ref.shape
    near = jnp.abs(iota(shape, 0) % NB - iota(shape, 1)) <= SMOOTH
    out_ref[...] = jnp.where(near | (iota(shape, 1) >= NB), 1.0, 0.0).astype(BF16)


def spectrum_kernel(core_ref, taps_ref, table_ref, sum_ref, raw_ref, keep_ref, give_ref, rows_ref, mat_ref, sem):
    windows = raw_ref.shape[0]
    copies = [pltpu.make_async_copy(raw_ref.at[w], rows_ref.at[w], sem.at[w]) for w in range(windows)]
    for copy in copies:
        copy.start()
    taps = taps_ref[...].astype(F32)
    n = taps.shape[1]
    wide = jnp.concatenate([taps, jnp.zeros_like(taps)], axis=1)
    toeplitz = pltpu.roll(jnp.broadcast_to(wide, (n, 2 * n)), 0, 1, stride=1, stride_axis=0).astype(BF16)
    for b in range(mat_ref.shape[0] // n):
        mat_ref[b * n : (b + 1) * n, :] = dot(toeplitz, table_ref[b * n : (b + 2) * n, :]).astype(BF16)
    averaging = sum_ref[...]
    bins = iota((1, NB), 1)
    counts = jnp.minimum(bins, SMOOTH) + jnp.minimum(NB - 1 - bins, SMOOTH) + 1
    inverse = 1.0 / counts.astype(F32)
    first_core = core_ref[0] == 0
    half = NB // 2

    def whiten(w, spec):
        re, im = spec[:, :NB], spec[:, NB:]
        mag = jnp.sqrt(re * re + im * im)
        high = mag.astype(BF16)
        low = (mag - high.astype(F32)).astype(BF16)
        sums = dot(jnp.concatenate([high, low], axis=1), averaging)
        divisor = sums[:, :NB] * inverse + sums[:, NB:] * (0.1 / NB) + 1e-06
        scale = 1.0 / divisor
        re = re * scale
        im = im * scale
        left = iota(re.shape, 1) < half
        first = jnp.where(left, re, pltpu.roll(im, half, 1))
        second = jnp.where(left, pltpu.roll(re, half, 1), im)
        keep_ref[w] = jnp.where(first_core, first, second).astype(BF16)
        give_ref[w] = jnp.where(first_core, second, first).astype(BF16)

    for start in range(0, windows, 2):
        pair = range(start, min(start + 2, windows))
        for w in pair:
            copies[w].wait()
        specs = [dot(rows_ref[w], mat_ref[...]) for w in pair]
        for w, spec in zip(pair, specs):
            whiten(w, spec)


def lane_sum(value):
    return jnp.sum(value, axis=1, keepdims=True)


def mark_kernel(high_count, *refs):
    for pairs_ref, marks_ref in zip(refs[: len(refs) // 2], refs[len(refs) // 2 :]):
        mark(high_count, pairs_ref, marks_ref)


def mark(high_count, pairs_ref, marks_ref):
    table = None
    for j in range(2):
        ids = pairs_ref[j : j + 1, :]
        high = (iota((high_count, ids.shape[1]), 0) == ids // LANES).astype(F32).astype(BF16)
        low = (iota((LANES, ids.shape[1]), 0) == ids % LANES).astype(F32).astype(BF16)
        part = dot(high, low, NT)
        table = part if table is None else table + part
    bits = jnp.where(table > 0.5, 1, 0) << (iota(table.shape, 0) % 32)
    for w in range(marks_ref.shape[1] // LANES):
        word = bits[32 * w : min(32 * w + 32, high_count), :]
        marks_ref[:, w * LANES : (w + 1) * LANES] = jnp.sum(word, axis=0, keepdims=True)


def wanted(marks, ids):
    parts = []
    words = marks.shape[1] // LANES
    for g in range(ids.shape[1] // LANES):
        here = ids[:, g * LANES : (g + 1) * LANES]
        high, low = here // LANES, here % LANES
        found = jnp.zeros_like(here)
        for w in range(words):
            word = jnp.take_along_axis(marks[:, w * LANES : (w + 1) * LANES], low, axis=1)
            found = jnp.where(high // 32 == w, word, found)
        parts.append((found >> (high % 32)) & 1)
    return parts


def places(parts):
    ahead = (iota((LANES, LANES), 0) < iota((LANES, LANES), 1)).astype(F32).astype(BF16)
    count = None
    out = []
    for part in parts:
        value = part.astype(F32)
        place = dot(value.astype(BF16), ahead)
        if count is not None:
            place = place + count
        out.append(jnp.where(part > 0, place, -1.0).astype(I32))
        total = lane_sum(value)
        count = total if count is None else count + total
    return jnp.concatenate(out, axis=1), count


def padded(chunk):
    return -(-chunk // 8) * 8


def folded(chunk, width):
    fold = 1
    while chunk * fold % 8:
        fold *= 2
    return chunk * fold, width // fold


def lay_out(chunk, chunk_refs, rows_ref):
    stride, part = padded(chunk), chunk_refs[0].shape[1]
    for k, ref in enumerate(chunk_refs):
        for p in range(rows_ref.shape[1] // part):
            rows_ref[k * stride : k * stride + chunk, p * part : (p + 1) * part] = ref[p * chunk : (p + 1) * chunk, :]
        if stride > chunk:
            rows_ref[k * stride + chunk : (k + 1) * stride, :] = jnp.zeros((stride - chunk, rows_ref.shape[1]), BF16)


def spread(row, count):
    return jnp.broadcast_to(row, (count, row.shape[1]))


def stacked(refs):
    marks = jnp.concatenate([ref[...] for ref in refs], axis=0)
    pad = -marks.shape[0] % 8
    if pad:
        marks = jnp.concatenate([marks, jnp.zeros((pad, marks.shape[1]), I32)], axis=0)
    return marks


def pack_kernel(lines, pieces, chunk, me_ref, *refs):
    marks = stacked(refs[:pieces])
    chan_ref, keep_ref, other_ref = refs[pieces : pieces + 3]
    chunk_refs = refs[pieces + 3 :]
    part, stride = chunk_refs[0].shape[1], padded(chunk)
    rows = chan_ref.shape[1]
    ids = spread(chan_ref[pl.ds(me_ref[0], 1), :], marks.shape[0])
    place, _ = places(wanted(marks, ids))
    slots = iota((stride, rows), 0)
    select = [(slots == place[i : i + 1, :]).astype(F32).astype(BF16) for i in lines]
    select = jnp.concatenate(select, axis=0)
    for w in range(keep_ref.shape[0]):
        data = jnp.concatenate([keep_ref[w], other_ref[w]], axis=1)
        out = dot(select, data).astype(BF16)
        fold, lane = 2 * w * LANES // part * chunk, 2 * w * LANES % part
        for i in range(len(lines)):
            chunk_refs[i][fold : fold + chunk, lane : lane + 2 * LANES] = out[i * stride : i * stride + chunk]


def tables_kernel(n, me_ref, *refs):
    marks = stacked(refs[:-3])[:n]
    chan_ref, place_ref, rank_ref = refs[-3:]
    place_ref[...], _ = places(wanted(marks, spread(chan_ref[pl.ds(me_ref[0], 1), :], n)))
    rank_ref[...], _ = places(wanted(spread(marks[:1], n), chan_ref[...]))


def arrival_kernel(sources, chunk, pieces, me_ref, *refs):
    marks = stacked(refs[:pieces])
    chan_ref, pairs_ref, early_ref, late_ref, most_ref = refs[pieces:]
    n = len(sources)
    ids = jnp.concatenate([chan_ref[pl.ds(me_ref[0] ^ k, 1), :] for k in sources], axis=0)
    most = None
    for k in range(n):
        parts = wanted(spread(marks[k : k + 1, :], n), ids)
        if k == 0:
            place, count = places(parts)
        else:
            count = lane_sum(sum(parts).astype(F32))
        most = count if most is None else jnp.maximum(most, count)
    most_ref[...] = jnp.max(most, axis=0, keepdims=True).astype(I32)
    stride = padded(chunk)
    slots = iota((stride, ids.shape[1]), 0)
    slots = jnp.where(slots < chunk, slots, -2)
    here = []
    for s in range(n):
        held = jnp.where(slots == place[s : s + 1, :], ids[s : s + 1, :] + 1, 0)
        here.append(lane_sum(held.astype(F32)))
    column = jnp.concatenate(here, axis=0) - 1.0
    row = jnp.broadcast_to(column, (n * stride, LANES)).T[:1, :]
    ends = pairs_ref[...].astype(F32)
    count = ends.shape[1]
    ends = jnp.concatenate([ends, jnp.zeros((6, count), F32)], axis=0).T
    middle = n // 2 * stride
    for j in range(2):
        match = ends[:, j : j + 1] == row
        match = jnp.where(match, 1.0, 0.0).astype(BF16)
        early_ref[j * count : (j + 1) * count, :] = match[:, :middle]
        late_ref[j * count : (j + 1) * count, :] = match[:, middle:]


def early_kernel(half, chunk, gather_ref, *refs):
    chunk_refs, out_ref, rows_ref = refs[:half], refs[half], refs[half + 1]
    lay_out(chunk, chunk_refs, rows_ref)
    for w in range(0, rows_ref.shape[1], 2 * LANES):
        out_ref[:, w : w + 2 * LANES] = dot(gather_ref[...], rows_ref[:, w : w + 2 * LANES]).astype(BF16)


def product_kernel(half, chunk, start, early_ref, gather_ref, *refs):
    chunk_refs, out_ref, rows_ref = refs[:half], refs[half], refs[half + 1]
    lay_out(chunk, chunk_refs, rows_ref)
    count = out_ref.shape[0]
    total = gather_ref.shape[0] // 2
    pick = jnp.concatenate([gather_ref[start : start + count, :], gather_ref[total + start : total + start + count, :]])
    middle = LANES // 2
    straight = crossed = None
    for w in range(0, rows_ref.shape[1] // LANES, 2):
        ends = dot(pick, rows_ref[:, w * LANES : (w + 2) * LANES])
        for v in range(2):
            lanes = slice((w + v) * LANES, (w + v + 1) * LANES)
            a = ends[:count, v * LANES : (v + 1) * LANES] + early_ref[start : start + count, lanes].astype(F32)
            b = ends[count:, v * LANES : (v + 1) * LANES] + early_ref[total + start : total + start + count, lanes].astype(F32)
            turned = pltpu.roll(a, middle, 1)
            straight = a * b if straight is None else straight + a * b
            crossed = turned * b if crossed is None else crossed + turned * b
    real = straight + pltpu.roll(straight, middle, 1)
    imag = pltpu.roll(crossed, middle, 1) - crossed
    out_ref[...] = jnp.where(iota(real.shape, 1) < middle, real, imag).astype(out_ref.dtype)


def finish_kernel(factor, core_ref, *refs):
    parts = (len(refs) - 1) // 2
    out_ref = refs[-1]
    first_core = core_ref[0] == 0
    half = LANES // 2
    start = 0
    for i in range(parts):
        mine = refs[i][...] * factor
        other = refs[parts + i][...] * factor
        first = jnp.where(first_core, mine, other)
        second = jnp.where(first_core, other, mine)
        left = iota(first.shape, 1) < half
        here = slice(start, start + first.shape[0])
        start += first.shape[0]
        out_ref[here, :LANES] = jnp.where(left, first, pltpu.roll(second, half, 1))
        out_ref[here, LANES:] = jnp.where(left, pltpu.roll(first, half, 1), second)


def swap(value, axis, size, bit):
    return lax.ppermute(value, axis, [(i, i ^ bit) for i in range(size)])


def call(kernel, out, flops=0, scratch=(), smem=1):
    def run(*args):
        many = isinstance(out, (tuple, list))
        specs = [SMEM] * smem + [VMEM] * (len(args) - smem)
        outs = list(out) if many else [out]
        size = sum(a.size * a.dtype.itemsize for a in args) + sum(o.size * o.dtype.itemsize for o in outs)
        return pl.pallas_call(
            kernel,
            out_shape=tuple(out) if many else out,
            in_specs=specs,
            out_specs=(VMEM,) * len(outs) if many else VMEM,
            scratch_shapes=scratch,
            compiler_params=pltpu.CompilerParams(vmem_limit_bytes=24 * 1024 * 1024),
            cost_estimate=pl.CostEstimate(flops=flops, bytes_accessed=size, transcendentals=0),
        )(*args)

    return run


def spectra(tm, core, raw_blocks, fir_taps):
    windows, rows, length = raw_blocks.shape
    table = jnp.asarray(table_of(length, fir_taps.shape[0]))
    shape = jax.ShapeDtypeStruct((2 * NB, 2 * NB), BF16)
    averaging = call(averaging_kernel, shape, flops=FIRST_FLOPS)(core)
    half = jax.ShapeDtypeStruct((windows, rows, NB), BF16)
    keep, give = pl.pallas_call(
        spectrum_kernel,
        out_shape=(half, half),
        in_specs=[SMEM, VMEM, VMEM, VMEM, pl.BlockSpec(memory_space=pl.ANY)],
        out_specs=(VMEM, VMEM),
        scratch_shapes=[
            pltpu.VMEM(raw_blocks.shape, BF16),
            pltpu.VMEM((length, 2 * NB), BF16),
            pltpu.SemaphoreType.DMA((windows,)),
        ],
        compiler_params=pltpu.CompilerParams(vmem_limit_bytes=24 * 1024 * 1024),
        cost_estimate=pl.CostEstimate(
            flops=2 * windows * rows * length * 2 * NB, bytes_accessed=2 * windows * rows * length, transcendentals=0
        ),
    )(core, fir_taps.reshape(1, -1), table, averaging, raw_blocks)
    return keep, swap(give, "tm", tm, 1)


def all_rounds(tm, n, chunk, order, me, core, raw_blocks, fir_taps, by_block, pairs, marks, most):
    windows, rows, _ = raw_blocks.shape
    pair_count = pairs.shape[0]
    width = 2 * windows * LANES
    data = jnp.concatenate(spectra(tm, core, raw_blocks, fir_taps), axis=0)
    data = data.transpose(1, 0, 2).reshape(rows, width)
    tables = [jax.ShapeDtypeStruct((n, rows), I32)] * 2
    place, rank = call(functools.partial(tables_kernel, n), tables)(me, *marks, by_block)
    place = jnp.stack([place[order.index(k)] for k in range(n)])
    held = jnp.where(rank < 0, 0, 1)
    relative = jnp.arange(n, dtype=I32) ^ me[0]
    counts = jnp.sum(held, axis=1)[relative]
    offsets = jnp.cumsum(counts) - counts
    line_of_row = (offsets[relative][:, None] + rank).reshape(-1)
    ends = pairs.T.reshape(-1)
    line = jnp.sum(jnp.where(ends[:, None] == by_block.reshape(1, -1), line_of_row[None, :], 0), axis=1)
    lines = jnp.arange(n * chunk, dtype=I32)

    def again(inner):
        done, merged = inner
        slot = jnp.arange(chunk, dtype=I32) + done
        select = (slot[None, :, None] == place[:, None, :]).astype(BF16).reshape(n * chunk, rows)
        packed = dot(select, data).astype(BF16)
        new = [packed[k * chunk : (k + 1) * chunk] for k in range(n)]
        new = jnp.concatenate([swap(new[k], "chan", n, k) if k else new[k] for k in range(n)])
        target = jnp.where(slot[None, :] < counts[:, None], offsets[:, None] + slot[None, :], -1).reshape(1, -1)
        return done + chunk, merged + dot((lines[:, None] == target).astype(BF16), new).astype(BF16)

    start = (jnp.int32(0), jnp.zeros((n * chunk, width), BF16))
    _, merged = lax.while_loop(lambda inner: inner[0] < most[0, 0], again, start)
    taken = dot((lines[None, :] == line[:, None]).astype(BF16), merged)
    taken = taken.reshape(2, pair_count, 2 * windows, 2, LANES // 2)
    a, b = taken[0], taken[1]
    real = jnp.sum(a[:, :, 0] * b[:, :, 0] + a[:, :, 1] * b[:, :, 1], axis=1)
    imag = jnp.sum(a[:, :, 1] * b[:, :, 0] - a[:, :, 0] * b[:, :, 1], axis=1)
    total = jnp.concatenate([real, imag], axis=1)
    bit = 2
    while bit < tm:
        total = total + swap(total, "tm", tm, bit)
        bit *= 2
    return finish(core, tm, windows, [total], [swap(total, "tm", tm, 1)])


def finish(core, tm, windows, mine, other):
    rows = sum(value.shape[0] for value in mine)
    kernel = functools.partial(finish_kernel, 1.0 / (windows * tm))
    return call(kernel, jax.ShapeDtypeStruct((rows, 2 * LANES), F32))(core, *mine, *other)


def steps_of(n):
    bits = [n // 2] + [1 << i for i in range(n.bit_length() - 2)]
    order, known = [0], []
    for bit in bits:
        known.append([k ^ bit for k in order])
        order = order + known[-1]
    return bits, known, order


def arrivals(n):
    _, known, _ = steps_of(n)
    far = [k for ks in known for k in sorted(ks) if k >= n // 2]
    near = list(range(n // 2 - 1, 0, -1))
    sends = SENDS if n == 8 else far[:-1] + near + far[-1:]
    early = EARLY if n == 8 else [0] + sends[: n // 2 - 1]
    return sends, early, [k for k in sends if k not in early]


def local(tm, n, raw_blocks, fir_taps, recorder_channel, pairs):
    windows, rows, _ = raw_blocks.shape
    pair_count = pairs.shape[0]
    chunk = ROUND_ROWS
    half = n // 2
    high_count = n * rows // LANES
    shaped = jax.ShapeDtypeStruct
    me = lax.axis_index("chan").astype(I32).reshape(1)
    core = (lax.axis_index("tm") % 2).astype(I32).reshape(1)
    by_block = recorder_channel.reshape(n, rows)
    width = 2 * windows * LANES
    bits, known, order = steps_of(n)
    _, early, late = arrivals(n)

    mark_shape = shaped((1, -(-high_count // 32) * LANES), I32)
    keep, other = spectra(tm, core, raw_blocks, fir_taps)
    theirs = swap(pairs.T, "chan", n, bits[0])
    own, new = call(functools.partial(mark_kernel, high_count), [mark_shape] * 2, smem=0)(pairs.T, theirs)

    marks = [own]
    arrived = [None] * n
    for i, bit in enumerate(bits):
        if i:
            new = swap(jnp.concatenate(marks), "chan", n, bit)
        here = [new] if i else [new, own]
        marks.append(new)
        owners = known[i] if i else known[i] + [0]
        kernel = functools.partial(pack_kernel, list(range(len(owners))), len(here), chunk)
        packed = call(kernel, [shaped(folded(chunk, width), BF16)] * len(owners))(me, *here, by_block, keep, other)
        for k, value in zip(owners, packed):
            arrived[k] = swap(value, "chan", n, k) if k else value

    shapes = [shaped((2 * pair_count, half * padded(chunk)), BF16)] * 2 + [shaped((1, 1), I32)]
    kernel = functools.partial(arrival_kernel, early + late, chunk, len(marks))
    pick_early, pick_late, most = call(kernel, shapes)(me, *marks, by_block, pairs.T)
    scratch = [pltpu.VMEM((half * padded(chunk), width), BF16)]
    found = call(
        functools.partial(early_kernel, half, chunk),
        shaped((2 * pair_count, width), BF16),
        flops=4 * pair_count * half * chunk * width,
        scratch=scratch,
        smem=0,
    )(pick_early, *[arrived[k] for k in early])

    sizes = [pair_count * 5 // 8, pair_count * 3 // 8]
    totals, seconds = [], []
    for i, size in enumerate(sizes):
        total = call(
            functools.partial(product_kernel, half, chunk, sum(sizes[:i])),
            shaped((size, LANES), BF16),
            flops=4 * size * half * chunk * width,
            scratch=scratch,
            smem=0,
        )(found, pick_late, *[arrived[k] for k in late])
        bit = 2
        while bit < tm:
            sent = total.astype(BF16)
            total = sent.astype(F32) + swap(sent, "tm", tm, bit).astype(F32)
            bit *= 2
        totals.append(total.astype(F32))
    for total in totals:
        seconds.append(swap(total, "tm", tm, 1))
    result = finish(core, tm, windows, totals, seconds)

    def rounds(state):
        given = lax.optimization_barrier((state[0], me, core, raw_blocks, fir_taps, by_block, pairs, marks, most))
        return jnp.int32(0), all_rounds(tm, n, chunk, order, *given[1:])

    more = jnp.where(most[0, 0] > chunk, 1, 0)
    return lax.while_loop(lambda state: state[0] > 0, rounds, (more, result))[1]


def solution(mesh):
    tm, n = mesh.shape["tm"], mesh.shape["chan"]
    in_specs = (P("tm", "chan", None), P(), P(), P("chan", None))
    out_specs = P("chan", None)

    def body(*args):
        return local(tm, n, *args)

    return jax.shard_map(body, mesh=mesh, in_specs=in_specs, out_specs=out_specs, check_vma=False)
```

```python
import functools

import jax
import jax.numpy as jnp
import ml_dtypes
import numpy as np
from jax import lax
from jax.experimental import pallas as pl
from jax.experimental.pallas import tpu as pltpu
from jax.sharding import PartitionSpec as P

NB = 128
SMOOTH = 4
LANES = 128
FIRST_FLOPS = 2 * 10**10
SENDS = [4, 1, 5, 3, 6, 2, 7]
EARLY = [0, 4, 1, 5]
ROUND_ROWS = 52

F32, BF16, I32 = jnp.float32, jnp.bfloat16, jnp.int32
VMEM = pl.BlockSpec(memory_space=pltpu.VMEM)
SMEM = pl.BlockSpec(memory_space=pltpu.SMEM)
NT = (((1,), (1,)), ((), ()))


def table_of(length, pad):
    samples = np.arange(length, dtype=np.int64)
    freqs = np.arange(1, NB + 1, dtype=np.int64)
    phase = (samples[:, None] * freqs[None, :] % length).astype(np.float32)
    angles = (phase * np.float32(2.0 * np.pi / length)).astype(np.float64)
    table = np.concatenate([np.cos(angles), -np.sin(angles)], axis=1).astype(np.float32)
    table = np.concatenate([table, np.zeros((pad, 2 * NB), np.float32)])
    return table.astype(ml_dtypes.bfloat16)


def dot(a, b, dims=(((1,), (0,)), ((), ()))):
    return lax.dot_general(a, b, dims, preferred_element_type=F32)


def iota(shape, axis):
    return lax.broadcasted_iota(I32, shape, axis)


def averaging_kernel(core_ref, out_ref):
    shape = out_ref.shape
    near = jnp.abs(iota(shape, 0) % NB - iota(shape, 1)) <= SMOOTH
    out_ref[...] = jnp.where(near | (iota(shape, 1) >= NB), 1.0, 0.0).astype(BF16)


def spectrum_kernel(core_ref, taps_ref, table_ref, sum_ref, raw_ref, keep_ref, give_ref, rows_ref, mat_ref, sem):
    windows = raw_ref.shape[0]
    copies = [pltpu.make_async_copy(raw_ref.at[w], rows_ref.at[w], sem.at[w]) for w in range(windows)]
    for copy in copies:
        copy.start()
    taps = taps_ref[...].astype(F32)
    n = taps.shape[1]
    wide = jnp.concatenate([taps, jnp.zeros_like(taps)], axis=1)
    toeplitz = pltpu.roll(jnp.broadcast_to(wide, (n, 2 * n)), 0, 1, stride=1, stride_axis=0).astype(BF16)
    for b in range(mat_ref.shape[0] // n):
        mat_ref[b * n : (b + 1) * n, :] = dot(toeplitz, table_ref[b * n : (b + 2) * n, :]).astype(BF16)
    averaging = sum_ref[...]
    bins = iota((1, NB), 1)
    counts = jnp.minimum(bins, SMOOTH) + jnp.minimum(NB - 1 - bins, SMOOTH) + 1
    inverse = 1.0 / counts.astype(F32)
    first_core = core_ref[0] == 0
    half = NB // 2

    def whiten(w, spec):
        re, im = spec[:, :NB], spec[:, NB:]
        mag = jnp.sqrt(re * re + im * im)
        high = mag.astype(BF16)
        low = (mag - high.astype(F32)).astype(BF16)
        sums = dot(jnp.concatenate([high, low], axis=1), averaging)
        divisor = sums[:, :NB] * inverse + sums[:, NB:] * (0.1 / NB) + 1e-06
        scale = 1.0 / divisor
        re = re * scale
        im = im * scale
        left = iota(re.shape, 1) < half
        first = jnp.where(left, re, pltpu.roll(im, half, 1))
        second = jnp.where(left, pltpu.roll(re, half, 1), im)
        keep_ref[w] = jnp.where(first_core, first, second).astype(BF16)
        give_ref[w] = jnp.where(first_core, second, first).astype(BF16)

    for start in range(0, windows, 4):
        pair = range(start, min(start + 4, windows))
        for w in pair:
            copies[w].wait()
        specs = [dot(rows_ref[w], mat_ref[...]) for w in pair]
        for w, spec in zip(pair, specs):
            whiten(w, spec)


def lane_sum(value):
    return jnp.sum(value, axis=1, keepdims=True)


def mark_kernel(high_count, *refs):
    for pairs_ref, marks_ref in zip(refs[: len(refs) // 2], refs[len(refs) // 2 :]):
        mark(high_count, pairs_ref, marks_ref)


def mark(high_count, pairs_ref, marks_ref):
    table = None
    for j in range(2):
        ids = pairs_ref[j : j + 1, :]
        high = (iota((high_count, ids.shape[1]), 0) == ids // LANES).astype(F32).astype(BF16)
        low = (iota((LANES, ids.shape[1]), 0) == ids % LANES).astype(F32).astype(BF16)
        part = dot(high, low, NT)
        table = part if table is None else table + part
    bits = jnp.where(table > 0.5, 1, 0) << (iota(table.shape, 0) % 32)
    for w in range(marks_ref.shape[1] // LANES):
        word = bits[32 * w : min(32 * w + 32, high_count), :]
        marks_ref[:, w * LANES : (w + 1) * LANES] = jnp.sum(word, axis=0, keepdims=True)


def wanted(marks, ids):
    parts = []
    words = marks.shape[1] // LANES
    for g in range(ids.shape[1] // LANES):
        here = ids[:, g * LANES : (g + 1) * LANES]
        high, low = here // LANES, here % LANES
        found = jnp.zeros_like(here)
        for w in range(words):
            word = jnp.take_along_axis(marks[:, w * LANES : (w + 1) * LANES], low, axis=1)
            found = jnp.where(high // 32 == w, word, found)
        parts.append((found >> (high % 32)) & 1)
    return parts


def places(parts):
    ahead = (iota((LANES, LANES), 0) < iota((LANES, LANES), 1)).astype(F32).astype(BF16)
    count = None
    out = []
    for part in parts:
        value = part.astype(F32)
        place = dot(value.astype(BF16), ahead)
        if count is not None:
            place = place + count
        out.append(jnp.where(part > 0, place, -1.0).astype(I32))
        total = lane_sum(value)
        count = total if count is None else count + total
    return jnp.concatenate(out, axis=1), count


def padded(chunk):
    return -(-chunk // 8) * 8


def folded(chunk, width):
    fold = 1
    while chunk * fold % 8:
        fold *= 2
    return chunk * fold, width // fold


def lay_out(chunk, chunk_refs, rows_ref):
    stride, part = padded(chunk), chunk_refs[0].shape[1]
    for k, ref in enumerate(chunk_refs):
        for p in range(rows_ref.shape[1] // part):
            rows_ref[k * stride : k * stride + chunk, p * part : (p + 1) * part] = ref[p * chunk : (p + 1) * chunk, :]
        if stride > chunk:
            rows_ref[k * stride + chunk : (k + 1) * stride, :] = jnp.zeros((stride - chunk, rows_ref.shape[1]), BF16)


def spread(row, count):
    return jnp.broadcast_to(row, (count, row.shape[1]))


def stacked(refs):
    marks = jnp.concatenate([ref[...] for ref in refs], axis=0)
    pad = -marks.shape[0] % 8
    if pad:
        marks = jnp.concatenate([marks, jnp.zeros((pad, marks.shape[1]), I32)], axis=0)
    return marks


def pack_kernel(lines, pieces, chunk, me_ref, *refs):
    marks = stacked(refs[:pieces])
    chan_ref, keep_ref, other_ref = refs[pieces : pieces + 3]
    chunk_refs = refs[pieces + 3 :]
    part, stride = chunk_refs[0].shape[1], padded(chunk)
    rows = chan_ref.shape[1]
    ids = spread(chan_ref[pl.ds(me_ref[0], 1), :], marks.shape[0])
    place, _ = places(wanted(marks, ids))
    slots = iota((stride, rows), 0)
    select = [(slots == place[i : i + 1, :]).astype(F32).astype(BF16) for i in lines]
    select = jnp.concatenate(select, axis=0)
    for w in range(keep_ref.shape[0]):
        data = jnp.concatenate([keep_ref[w], other_ref[w]], axis=1)
        out = dot(select, data).astype(BF16)
        fold, lane = 2 * w * LANES // part * chunk, 2 * w * LANES % part
        for i in range(len(lines)):
            chunk_refs[i][fold : fold + chunk, lane : lane + 2 * LANES] = out[i * stride : i * stride + chunk]


def tables_kernel(n, me_ref, *refs):
    marks = stacked(refs[:-3])[:n]
    chan_ref, place_ref, rank_ref = refs[-3:]
    place_ref[...], _ = places(wanted(marks, spread(chan_ref[pl.ds(me_ref[0], 1), :], n)))
    rank_ref[...], _ = places(wanted(spread(marks[:1], n), chan_ref[...]))


def arrival_kernel(sources, chunk, pieces, me_ref, *refs):
    marks = stacked(refs[:pieces])
    chan_ref, pairs_ref, early_ref, late_ref, most_ref = refs[pieces:]
    n = len(sources)
    ids = jnp.concatenate([chan_ref[pl.ds(me_ref[0] ^ k, 1), :] for k in sources], axis=0)
    most = None
    for k in range(n):
        parts = wanted(spread(marks[k : k + 1, :], n), ids)
        if k == 0:
            place, count = places(parts)
        else:
            count = lane_sum(sum(parts).astype(F32))
        most = count if most is None else jnp.maximum(most, count)
    most_ref[...] = jnp.max(most, axis=0, keepdims=True).astype(I32)
    stride = padded(chunk)
    slots = iota((stride, ids.shape[1]), 0)
    slots = jnp.where(slots < chunk, slots, -2)
    here = []
    for s in range(n):
        held = jnp.where(slots == place[s : s + 1, :], ids[s : s + 1, :] + 1, 0)
        here.append(lane_sum(held.astype(F32)))
    column = jnp.concatenate(here, axis=0) - 1.0
    row = jnp.broadcast_to(column, (n * stride, LANES)).T[:1, :]
    ends = pairs_ref[...].astype(F32)
    count = ends.shape[1]
    ends = jnp.concatenate([ends, jnp.zeros((6, count), F32)], axis=0).T
    middle = n // 2 * stride
    for j in range(2):
        match = ends[:, j : j + 1] == row
        match = jnp.where(match, 1.0, 0.0).astype(BF16)
        early_ref[j * count : (j + 1) * count, :] = match[:, :middle]
        late_ref[j * count : (j + 1) * count, :] = match[:, middle:]


def early_kernel(half, chunk, gather_ref, *refs):
    chunk_refs, out_ref, rows_ref = refs[:half], refs[half], refs[half + 1]
    lay_out(chunk, chunk_refs, rows_ref)
    for w in range(0, rows_ref.shape[1], 2 * LANES):
        out_ref[:, w : w + 2 * LANES] = dot(gather_ref[...], rows_ref[:, w : w + 2 * LANES]).astype(BF16)


def product_kernel(half, chunk, start, early_ref, gather_ref, *refs):
    chunk_refs, out_ref, rows_ref = refs[:half], refs[half], refs[half + 1]
    lay_out(chunk, chunk_refs, rows_ref)
    count = out_ref.shape[0]
    total = gather_ref.shape[0] // 2
    pick = jnp.concatenate([gather_ref[start : start + count, :], gather_ref[total + start : total + start + count, :]])
    middle = LANES // 2
    straight = crossed = None
    for w in range(0, rows_ref.shape[1] // LANES, 2):
        ends = dot(pick, rows_ref[:, w * LANES : (w + 2) * LANES])
        for v in range(2):
            lanes = slice((w + v) * LANES, (w + v + 1) * LANES)
            a = ends[:count, v * LANES : (v + 1) * LANES] + early_ref[start : start + count, lanes].astype(F32)
            b = ends[count:, v * LANES : (v + 1) * LANES] + early_ref[total + start : total + start + count, lanes].astype(F32)
            turned = pltpu.roll(a, middle, 1)
            straight = a * b if straight is None else straight + a * b
            crossed = turned * b if crossed is None else crossed + turned * b
    real = straight + pltpu.roll(straight, middle, 1)
    imag = pltpu.roll(crossed, middle, 1) - crossed
    out_ref[...] = jnp.where(iota(real.shape, 1) < middle, real, imag).astype(out_ref.dtype)


def finish_kernel(factor, core_ref, *refs):
    parts = (len(refs) - 1) // 2
    out_ref = refs[-1]
    first_core = core_ref[0] == 0
    half = LANES // 2
    start = 0
    for i in range(parts):
        mine = refs[i][...] * factor
        other = refs[parts + i][...] * factor
        first = jnp.where(first_core, mine, other)
        second = jnp.where(first_core, other, mine)
        left = iota(first.shape, 1) < half
        here = slice(start, start + first.shape[0])
        start += first.shape[0]
        out_ref[here, :LANES] = jnp.where(left, first, pltpu.roll(second, half, 1))
        out_ref[here, LANES:] = jnp.where(left, pltpu.roll(first, half, 1), second)


def swap(value, axis, size, bit):
    return lax.ppermute(value, axis, [(i, i ^ bit) for i in range(size)])


def call(kernel, out, flops=0, scratch=(), smem=1):
    def run(*args):
        many = isinstance(out, (tuple, list))
        specs = [SMEM] * smem + [VMEM] * (len(args) - smem)
        outs = list(out) if many else [out]
        size = sum(a.size * a.dtype.itemsize for a in args) + sum(o.size * o.dtype.itemsize for o in outs)
        return pl.pallas_call(
            kernel,
            out_shape=tuple(out) if many else out,
            in_specs=specs,
            out_specs=(VMEM,) * len(outs) if many else VMEM,
            scratch_shapes=scratch,
            compiler_params=pltpu.CompilerParams(vmem_limit_bytes=24 * 1024 * 1024),
            cost_estimate=pl.CostEstimate(flops=flops, bytes_accessed=size, transcendentals=0),
        )(*args)

    return run


def spectra(tm, core, raw_blocks, fir_taps):
    windows, rows, length = raw_blocks.shape
    table = jnp.asarray(table_of(length, fir_taps.shape[0]))
    shape = jax.ShapeDtypeStruct((2 * NB, 2 * NB), BF16)
    averaging = call(averaging_kernel, shape, flops=FIRST_FLOPS)(core)
    half = jax.ShapeDtypeStruct((windows, rows, NB), BF16)
    keep, give = pl.pallas_call(
        spectrum_kernel,
        out_shape=(half, half),
        in_specs=[SMEM, VMEM, VMEM, VMEM, pl.BlockSpec(memory_space=pl.ANY)],
        out_specs=(VMEM, VMEM),
        scratch_shapes=[
            pltpu.VMEM(raw_blocks.shape, BF16),
            pltpu.VMEM((length, 2 * NB), BF16),
            pltpu.SemaphoreType.DMA((windows,)),
        ],
        compiler_params=pltpu.CompilerParams(vmem_limit_bytes=24 * 1024 * 1024),
        cost_estimate=pl.CostEstimate(
            flops=2 * windows * rows * length * 2 * NB, bytes_accessed=2 * windows * rows * length, transcendentals=0
        ),
    )(core, fir_taps.reshape(1, -1), table, averaging, raw_blocks)
    return keep, swap(give, "tm", tm, 1)


def all_rounds(tm, n, chunk, order, me, core, raw_blocks, fir_taps, by_block, pairs, marks, most):
    windows, rows, _ = raw_blocks.shape
    pair_count = pairs.shape[0]
    width = 2 * windows * LANES
    data = jnp.concatenate(spectra(tm, core, raw_blocks, fir_taps), axis=0)
    data = data.transpose(1, 0, 2).reshape(rows, width)
    tables = [jax.ShapeDtypeStruct((n, rows), I32)] * 2
    place, rank = call(functools.partial(tables_kernel, n), tables)(me, *marks, by_block)
    place = jnp.stack([place[order.index(k)] for k in range(n)])
    held = jnp.where(rank < 0, 0, 1)
    relative = jnp.arange(n, dtype=I32) ^ me[0]
    counts = jnp.sum(held, axis=1)[relative]
    offsets = jnp.cumsum(counts) - counts
    line_of_row = (offsets[relative][:, None] + rank).reshape(-1)
    ends = pairs.T.reshape(-1)
    line = jnp.sum(jnp.where(ends[:, None] == by_block.reshape(1, -1), line_of_row[None, :], 0), axis=1)
    lines = jnp.arange(n * chunk, dtype=I32)

    def again(inner):
        done, merged = inner
        slot = jnp.arange(chunk, dtype=I32) + done
        select = (slot[None, :, None] == place[:, None, :]).astype(BF16).reshape(n * chunk, rows)
        packed = dot(select, data).astype(BF16)
        new = [packed[k * chunk : (k + 1) * chunk] for k in range(n)]
        new = jnp.concatenate([swap(new[k], "chan", n, k) if k else new[k] for k in range(n)])
        target = jnp.where(slot[None, :] < counts[:, None], offsets[:, None] + slot[None, :], -1).reshape(1, -1)
        return done + chunk, merged + dot((lines[:, None] == target).astype(BF16), new).astype(BF16)

    start = (jnp.int32(0), jnp.zeros((n * chunk, width), BF16))
    _, merged = lax.while_loop(lambda inner: inner[0] < most[0, 0], again, start)
    taken = dot((lines[None, :] == line[:, None]).astype(BF16), merged)
    taken = taken.reshape(2, pair_count, 2 * windows, 2, LANES // 2)
    a, b = taken[0], taken[1]
    real = jnp.sum(a[:, :, 0] * b[:, :, 0] + a[:, :, 1] * b[:, :, 1], axis=1)
    imag = jnp.sum(a[:, :, 1] * b[:, :, 0] - a[:, :, 0] * b[:, :, 1], axis=1)
    total = jnp.concatenate([real, imag], axis=1)
    bit = 2
    while bit < tm:
        total = total + swap(total, "tm", tm, bit)
        bit *= 2
    return finish(core, tm, windows, [total], [swap(total, "tm", tm, 1)])


def finish(core, tm, windows, mine, other):
    rows = sum(value.shape[0] for value in mine)
    kernel = functools.partial(finish_kernel, 1.0 / (windows * tm))
    return call(kernel, jax.ShapeDtypeStruct((rows, 2 * LANES), F32))(core, *mine, *other)


def steps_of(n):
    bits = [n // 2] + [1 << i for i in range(n.bit_length() - 2)]
    order, known = [0], []
    for bit in bits:
        known.append([k ^ bit for k in order])
        order = order + known[-1]
    return bits, known, order


def arrivals(n):
    _, known, _ = steps_of(n)
    far = [k for ks in known for k in sorted(ks) if k >= n // 2]
    near = list(range(n // 2 - 1, 0, -1))
    sends = SENDS if n == 8 else far[:-1] + near + far[-1:]
    early = EARLY if n == 8 else [0] + sends[: n // 2 - 1]
    return sends, early, [k for k in sends if k not in early]


def local(tm, n, raw_blocks, fir_taps, recorder_channel, pairs):
    windows, rows, _ = raw_blocks.shape
    pair_count = pairs.shape[0]
    chunk = ROUND_ROWS
    half = n // 2
    high_count = n * rows // LANES
    shaped = jax.ShapeDtypeStruct
    me = lax.axis_index("chan").astype(I32).reshape(1)
    core = (lax.axis_index("tm") % 2).astype(I32).reshape(1)
    by_block = recorder_channel.reshape(n, rows)
    width = 2 * windows * LANES
    bits, known, order = steps_of(n)
    _, early, late = arrivals(n)

    mark_shape = shaped((1, -(-high_count // 32) * LANES), I32)
    keep, other = spectra(tm, core, raw_blocks, fir_taps)
    theirs = swap(pairs.T, "chan", n, bits[0])
    own, new = call(functools.partial(mark_kernel, high_count), [mark_shape] * 2, smem=0)(pairs.T, theirs)

    marks = [own]
    arrived = [None] * n
    for i, bit in enumerate(bits):
        if i:
            new = swap(jnp.concatenate(marks), "chan", n, bit)
        here = [new] if i else [new, own]
        marks.append(new)
        owners = known[i] if i else known[i] + [0]
        kernel = functools.partial(pack_kernel, list(range(len(owners))), len(here), chunk)
        packed = call(kernel, [shaped(folded(chunk, width), BF16)] * len(owners))(me, *here, by_block, keep, other)
        for k, value in zip(owners, packed):
            arrived[k] = swap(value, "chan", n, k) if k else value

    shapes = [shaped((2 * pair_count, half * padded(chunk)), BF16)] * 2 + [shaped((1, 1), I32)]
    kernel = functools.partial(arrival_kernel, early + late, chunk, len(marks))
    pick_early, pick_late, most = call(kernel, shapes)(me, *marks, by_block, pairs.T)
    scratch = [pltpu.VMEM((half * padded(chunk), width), BF16)]
    found = call(
        functools.partial(early_kernel, half, chunk),
        shaped((2 * pair_count, width), BF16),
        flops=4 * pair_count * half * chunk * width,
        scratch=scratch,
        smem=0,
    )(pick_early, *[arrived[k] for k in early])

    sizes = [pair_count * 3 // 4, pair_count // 4]
    totals, seconds = [], []
    for i, size in enumerate(sizes):
        total = call(
            functools.partial(product_kernel, half, chunk, sum(sizes[:i])),
            shaped((size, LANES), BF16),
            flops=4 * size * half * chunk * width,
            scratch=scratch,
            smem=0,
        )(found, pick_late, *[arrived[k] for k in late])
        bit = 2
        while bit < tm:
            sent = total.astype(BF16)
            total = sent.astype(F32) + swap(sent, "tm", tm, bit).astype(F32)
            bit *= 2
        totals.append(total.astype(F32))
    for total in totals:
        seconds.append(swap(total, "tm", tm, 1))
    result = finish(core, tm, windows, totals, seconds)

    def rounds(state):
        given = lax.optimization_barrier((state[0], me, core, raw_blocks, fir_taps, by_block, pairs, marks, most))
        return jnp.int32(0), all_rounds(tm, n, chunk, order, *given[1:])

    more = jnp.where(most[0, 0] > chunk, 1, 0)
    return lax.while_loop(lambda state: state[0] > 0, rounds, (more, result))[1]


def solution(mesh):
    tm, n = mesh.shape["tm"], mesh.shape["chan"]
    in_specs = (P("tm", "chan", None), P(), P(), P("chan", None))
    out_specs = P("chan", None)

    def body(*args):
        return local(tm, n, *args)

    return jax.shard_map(body, mesh=mesh, in_specs=in_specs, out_specs=out_specs, check_vma=False)
```
